128 devices in a mesh: seq: 16 (over z, y_hi, core), col: 4 (over x), batch: 2 (over y_lo).
Axes of the slice: x: 4, y: 4 (y_hi: 2, y_lo: 2; y = y_hi * 2 + y_lo), z: 4, core: 2. Of those that a mesh axis runs over, the one named last changes fastest.
Arguments:
- tokens: int32 [2, 1048576], P('batch', ('seq', 'col')), may hold values from 0 to 3
- stem_weight: bfloat16 [64, 768], replicated, may hold values from -1.5 to 1.5
- conv_weight: bfloat16 [3840, 768], replicated, may hold values from -0.09375 to 0.09375
- conv_bias: float32 [768], replicated, may hold values from -1 to 1
- up_weight: bfloat16 [768, 1536], replicated, may hold values from -0.21875 to 0.21875
- norm_gain: float32 [1536], replicated, may hold values from 0.1 to 1.9
- pair_weight: bfloat16 [1536, 64], replicated, may hold values from -0.15625 to 0.15625
- out_weight: bfloat16 [1024, 128], replicated, may hold values from -0.1875 to 0.1875
- cotangent: bfloat16 [2, 512, 512, 128], P('batch', 'seq', 'col'), may hold values from -24 to 24
- projection: float32 [768, 128], replicated, may hold values from -0.21875 to 0.21875
- buckets: int32 [3840], replicated, may hold values from 0 to 31
Outputs:
- input_grad: bfloat16 [2, 65536, 768], P('batch', ('seq', 'col'))
- embedding: float32 [2, 32, 128], P('batch')
The draws below stay inside these ranges and needn't reach their ends.
All inputs are finite; a program needn't handle non-finite values.
Results may differ from the reference program's by a relative error of at most 0.012.
Values may be sent and summed in bfloat16 or wider, within the bound.
No kernel may reach another device: no remote copies, remote signals or barrier semaphores. Data moves between devices by JAX's collectives and lax.ppermute only.
A program may use at most 128 MiB of HBM per device.

```python
import jax
import jax.numpy as jnp
from jax import lax

C = 768
CB = 1536
PC = 128
OP = 32
KERNEL = 5
PATCH = 16
POOL = 128
BUCKETS = 32
PROJ = 128
B = 2
BINS = 512
FINE = 65536
BP = 1048576
ROWB = 32


def with_ends(result, own_key, smallest, high):
    longest = result.shape.index(max(result.shape))
    spots = []
    for shift in (0, 1):
        where = [jax.random.randint(jax.random.fold_in(own_key, axis), (), 0, length) for axis, length in enumerate(result.shape)]
        where[longest] = (where[longest] + shift) % result.shape[longest]
        spots.append(tuple(where))
    return result.at[spots[0]].set(smallest).at[spots[1]].set(high)


def block_levels(rng, extent, shards, least, largest):
    factor_of, own = 1.0, jax.random.fold_in(rng, 6)
    for axis_at, blocks in shards:
        heights = jnp.exp(jax.random.uniform(jax.random.fold_in(own, axis_at), (blocks,), jnp.float32, least / len(shards), largest / len(shards)))
        factor_of = factor_of * jnp.repeat(heights, extent[axis_at] // blocks).reshape([-1 if axis == axis_at else 1 for axis in range(len(extent))])
    return factor_of


def bell_draw(rng, dims, scale, most, cuts=(), kind=jnp.bfloat16):
    drawn = jax.random.normal(rng, dims, jnp.float32) * scale
    if len(cuts) > 0:
        drawn = block_levels(rng, dims, cuts, -0.22, 0.18) * drawn
    return jnp.clip(drawn, min=-most, max=most).astype(kind)


def setup_inputs(seed: int = 0) -> dict:
    splits = jax.random.split(jax.random.key(seed), 12)
    return {
        "tokens": with_ends(jax.random.randint(splits[0], (B, BP), 0, 4), jax.random.fold_in(splits[0], 1), 0, 3).astype(jnp.int32),
        "stem_weight": bell_draw(splits[1], (PATCH * 4, C), PATCH ** -0.5, 1.5),
        "conv_weight": bell_draw(splits[2], (KERNEL * C, C), (KERNEL * C) ** -0.5, 0.09375),
        "conv_bias": jnp.clip(jax.random.uniform(splits[3], (C,), jnp.float32, -1.0, 1.0), -1.0, 1.0),
        "up_weight": bell_draw(splits[4], (C, CB), C ** -0.5, 0.21875),
        "norm_gain": jnp.clip(1.0 + 0.18 * jax.random.normal(splits[5], (CB,), jnp.float32), 0.1, 1.9),
        "pair_weight": bell_draw(splits[6], (CB, 2 * OP), CB ** -0.5, 0.15625),
        "out_weight": bell_draw(splits[7], (OP * OP, PC), (OP * OP) ** -0.5, 0.1875),
        "cotangent": bell_draw(splits[8], (B, BINS, BINS, PC), 4.0, 24.0, ((0, 2), (1, 16), (2, 4))),
        "projection": bell_draw(splits[9], (C, PROJ), C ** -0.5, 0.21875, (), jnp.float32),
        "buckets": with_ends(jax.random.randint(splits[10], (KERNEL * C,), 0, BUCKETS), jax.random.fold_in(splits[10], 1), 0, BUCKETS - 1).astype(jnp.int32),
    }


highest = lax.Precision.HIGHEST

def one_interval(bases, stem_weight, conv_weight, conv_bias, up_weight, norm_gain, pair_weight, out_weight, grid, projection, buckets):
    reach = (KERNEL - 1) // 2
    onehot = (bases.reshape(FINE, PATCH)[:, :, None] == jnp.arange(4, dtype=jnp.int32)).astype(jnp.bfloat16).reshape(FINE, PATCH * 4)
    embedded = jnp.dot(onehot, stem_weight, preferred_element_type=jnp.float32).astype(jnp.bfloat16)
    padded = jnp.pad(embedded, ((reach, reach), (0, 0)))
    taps = conv_weight.reshape(KERNEL, C, C)
    before = jnp.zeros((FINE, C), jnp.float32) + conv_bias
    for offset in range(KERNEL):
        before = before + jnp.dot(padded[offset:offset + FINE], taps[offset], preferred_element_type=jnp.float32)
    after, gelu_back = jax.vjp(jax.nn.gelu, before)
    pooled = lax.optimization_barrier(jnp.mean(after.reshape(BINS, POOL, C), axis=1)).astype(jnp.bfloat16)
    hidden = jnp.dot(pooled, up_weight, preferred_element_type=jnp.float32)
    inverse = lax.rsqrt(lax.optimization_barrier(jnp.mean(hidden * hidden, axis=1, keepdims=True)) + 1e-06)
    normed = (hidden * inverse * norm_gain).astype(jnp.bfloat16)
    left = jnp.dot(normed, pair_weight[:, :OP], preferred_element_type=jnp.float32).astype(jnp.bfloat16)
    right = jnp.dot(normed, pair_weight[:, OP:], preferred_element_type=jnp.float32).astype(jnp.bfloat16)
    groups = BINS // ROWB
    blocks = grid.reshape(groups, ROWB, BINS, PC)
    left_groups = left.astype(jnp.float32).reshape(groups, ROWB, OP)
    right_wide = right.astype(jnp.float32)

    def pair_step(carry, inputs):
        block, rows_left = inputs
        outer_grad = lax.dot_general(block.reshape(ROWB * BINS, PC), out_weight, (((1,), (1,)), ((), ())), preferred_element_type=jnp.float32).reshape(ROWB, BINS, OP, OP)
        grad_left = jnp.einsum('ijkl,jl->ik', outer_grad, right_wide, precision=highest)
        carry = carry + jnp.einsum('ijkl,ik->jl', outer_grad, rows_left, precision=highest)
        return (carry, grad_left)
    grad_right, grad_left = lax.scan(pair_step, jnp.zeros((BINS, OP), jnp.float32), (blocks, left_groups))
    grad_left = grad_left.reshape(BINS, OP)
    both_grads = jnp.concatenate([grad_left, grad_right], axis=1)
    d_normed = lax.dot_general(both_grads, pair_weight.astype(jnp.float32), (((1,), (1,)), ((), ())), precision=highest)
    scaled = d_normed * norm_gain
    inner = lax.optimization_barrier(jnp.mean(scaled * hidden, axis=1, keepdims=True))
    d_hidden = inverse * scaled - hidden * inverse ** 3 * inner
    d_pooled = lax.dot_general(d_hidden, up_weight.astype(jnp.float32), (((1,), (1,)), ((), ())), precision=highest)
    spread = jnp.broadcast_to(d_pooled[:, None, :] / POOL, (BINS, POOL, C)).reshape(FINE, C)
    d_before = gelu_back(spread)[0].astype(jnp.bfloat16)
    grads_padded = jnp.pad(d_before, ((reach, reach), (0, 0)))
    input_grad = jnp.zeros((FINE, C), jnp.float32)
    for offset in range(KERNEL):
        first = 2 * reach - offset
        input_grad = input_grad + lax.dot_general(grads_padded[first:first + FINE], taps[offset], (((1,), (1,)), ((), ())), preferred_element_type=jnp.float32)
    weight_grad = jnp.concatenate([lax.dot_general(padded[offset:offset + FINE], d_before, (((0,), (0,)), ((), ())), preferred_element_type=jnp.float32) for offset in range(KERNEL)], axis=0)
    member = (buckets[None, :] == jnp.arange(BUCKETS, dtype=jnp.int32)[:, None]).astype(jnp.float32)
    sketch = jnp.dot(member, jnp.dot(weight_grad, projection, precision=highest), precision=highest)
    unit = sketch * lax.rsqrt(jnp.mean(sketch * sketch) + 1e-06)
    return (input_grad.astype(jnp.bfloat16), unit)

def reference(tokens, stem_weight, conv_weight, conv_bias, up_weight, norm_gain, pair_weight, out_weight, cotangent, projection, buckets):
    grads_list = []
    units_list = []
    for interval in range(B):
        grads_one, unit_one = one_interval(tokens[interval], stem_weight, conv_weight, conv_bias, up_weight, norm_gain, pair_weight, out_weight, cotangent[interval], projection, buckets)
        grads_list.append(grads_one)
        units_list.append(unit_one)
    units = jnp.stack(units_list, axis=0)
    center = lax.optimization_barrier(jnp.sum(units, axis=0)) / B
    return (jnp.stack(grads_list, axis=0), units - center[None])
```

```python
import functools
import jax
import jax.numpy as jnp
from jax import lax
from jax.experimental import pallas as pl
from jax.experimental.pallas import tpu as pltpu
from jax.sharding import PartitionSpec as P

OP = 32
PATCH = 16
POOL = 128
BUCKETS = 32
LANES = 128
PAD = 8
ROOT = 0.7978845608028654
CUBIC = 0.044715

f32 = jnp.float32
bf16 = jnp.bfloat16
NT = (((1,), (1,)), ((), ()))
highest = lax.Precision.HIGHEST


def split(x):
    hi = lax.reduce_precision(x, 8, 7)
    return hi.astype(bf16), (x - hi).astype(bf16)


def split_rows(x):
    hi, lo = split(x)
    return jnp.concatenate([hi, lo], axis=0)


def split_in_kernel(x):
    hi = x.astype(bf16)
    return hi, (x - hi.astype(f32)).astype(bf16)


def pair_kernel(where, parts, cot, wide, out, moved):
    rows, cols, _ = cot.shape
    bins = parts.shape[1]
    seq, col = where[0], where[1]
    mine = parts[pl.ds(seq * (rows // bins), rows // bins)].astype(f32).reshape(rows, LANES)
    left = mine[:, :OP].astype(bf16)
    other = parts[pl.ds(col * (cols // bins), cols // bins)].astype(f32).reshape(cols, LANES)
    right = other.T[OP : 2 * OP].astype(bf16)
    grid = jnp.concatenate([cot[i] for i in range(rows)], axis=1)
    weighted = jnp.dot(left, wide[...], preferred_element_type=f32)
    for l in range(OP):
        moved[pl.ds(l, rows, stride=OP), :] = weighted[:, l * LANES : (l + 1) * LANES]
    stacked = jnp.concatenate([moved[i * OP : (i + 1) * OP, :] for i in range(rows)], axis=1)
    hi, lo = split_in_kernel(stacked)
    both = lax.dot_general(
        grid, jnp.concatenate([hi, lo], axis=0), NT, preferred_element_type=f32
    )
    grad_right = both[:, :OP] + both[:, OP:]
    summed = jnp.dot(right, grid, preferred_element_type=f32)
    for i in range(rows):
        moved[i * OP : (i + 1) * OP, :] = summed[:, i * LANES : (i + 1) * LANES]
    by_row = jnp.concatenate([moved[pl.ds(l, rows, stride=OP), :] for l in range(OP)], axis=1)
    hi, lo = split_in_kernel(by_row)
    both = lax.dot_general(
        jnp.concatenate([hi, lo], axis=0), wide[...], NT, preferred_element_type=f32
    )
    grad_left = both[:rows] + both[rows:]
    out[...] = jnp.zeros_like(out)
    out[pl.ds(seq * (rows // bins), rows // bins), :, :OP] = grad_left.reshape(-1, bins, OP)
    out[pl.ds(col * (cols // bins), cols // bins), :, OP : 2 * OP] = grad_right.reshape(
        -1, bins, OP
    )


def pair_stage(where, parts, cot, wide):
    vmem = pl.BlockSpec(memory_space=pltpu.VMEM)
    return pl.pallas_call(
        pair_kernel,
        out_shape=jax.ShapeDtypeStruct(parts.shape, f32),
        in_specs=[pl.BlockSpec(memory_space=pltpu.SMEM), vmem, vmem, vmem],
        out_specs=vmem,
        scratch_shapes=[pltpu.VMEM((cot.shape[0] * OP, LANES), f32)],
        compiler_params=pltpu.CompilerParams(vmem_limit_bytes=32 << 20),
        cost_estimate=pl.CostEstimate(flops=200_000_000, bytes_accessed=2_000_000, transcendentals=0),
        name="pair",
    )(where, parts, cot, wide)


def iota(shape, dim): return lax.broadcasted_iota(jnp.int32, shape, dim)

def forward_kernel(chunk, tokens, ends, stem, taps, bias, up, gain, pair, spread, slope, hidden_out, inverse_out, parts, cells, unfolded, pools):
    lines = tokens.shape[0]
    patches = lines * LANES // PATCH
    per = LANES // PATCH
    channels = stem.shape[1]
    blocks = channels // LANES
    kernel = taps.shape[0] // channels
    reach = (kernel - 1) // 2
    t = iota((patches, LANES), 0)
    lane = iota((patches, LANES), 1)
    repeat = (t // per == lane).astype(bf16)
    rows = jnp.dot(repeat, tokens[...].astype(f32).astype(bf16), preferred_element_type=f32)
    own = jnp.where(lane // PATCH == t % per, rows + 1.0, 0.0).astype(bf16)
    fold = (iota((LANES, 4 * PATCH), 0) % PATCH == iota((LANES, 4 * PATCH), 1) // 4).astype(bf16)
    base = jnp.dot(own, fold, preferred_element_type=f32)
    onehot = (base == (iota((patches, 4 * PATCH), 1) % 4 + 1).astype(f32)).astype(f32).astype(bf16)
    main = jnp.dot(onehot, stem[...], preferred_element_type=f32).astype(bf16)
    edges = jnp.dot(ends[...].astype(bf16), stem[...], preferred_element_type=f32).astype(bf16).astype(f32)
    spread[PAD:PAD + patches, :] = main
    wide = main.astype(f32)
    for c in range(blocks):
        at = slice(c * LANES, (c + 1) * LANES)
        cells[c, :PAD, :] = edges[:PAD, at]
        cells[c, PAD:PAD + patches, :] = wide[:, at]
        cells[c, PAD + patches:, :] = edges[PAD:, at]
    spread[:PAD, :] = edges[:PAD].astype(bf16)
    spread[PAD + patches:, :] = edges[PAD:].astype(bf16)
    for r in range(patches // chunk):
        slot = r % 2
        for k in range(kernel):
            for c in range(blocks):
                start = r * chunk + PAD - reach + k
                j = (k * blocks + c) * LANES
                unfolded[slot, :, j:j + LANES] = cells[c, start:start + chunk, :].astype(bf16)
        before = jnp.dot(unfolded[slot], taps[...], preferred_element_type=f32) + bias[...]
        square = before * before
        bent = jnp.tanh(before * (ROOT + ROOT * CUBIC * square))
        half = 0.5 * (1.0 + bent)
        after = before * half
        tilt = half + before * (0.5 - 0.5 * bent * bent) * (ROOT + 3.0 * ROOT * CUBIC * square)
        slope[r * chunk:(r + 1) * chunk, :] = tilt.astype(bf16)
        for n in range(chunk // POOL):
            b = r * (chunk // POOL) + n
            pools[b:b + 1, :] = jnp.sum(after[n * POOL:(n + 1) * POOL], axis=0, keepdims=True) * (1.0 / POOL)
    hidden = jnp.dot(pools[...].astype(bf16), up[...], preferred_element_type=f32)
    inverse = lax.rsqrt(jnp.mean(hidden * hidden, axis=1, keepdims=True) + 1e-06)
    normed = (hidden * inverse * gain[...]).astype(bf16)
    sides = lax.dot_general(normed, pair[...], NT, preferred_element_type=f32)
    hidden_out[...] = hidden
    inverse_out[...] = jnp.broadcast_to(inverse, inverse_out.shape)
    full = jnp.concatenate([sides, jnp.zeros_like(sides)], axis=1).astype(bf16)
    parts[...] = jnp.broadcast_to(full[None], parts.shape)

def forward_stage(tokens, ends, stem, taps, bias, up, gain, pair, count, chunk=256):
    vmem = pl.BlockSpec(memory_space=pltpu.VMEM)
    lines = tokens.shape[0]
    patches = lines * LANES // PATCH
    channels = stem.shape[1]
    bins = patches // POOL
    tall = patches + 2 * PAD
    return pl.pallas_call(
        functools.partial(forward_kernel, chunk),
        out_shape=[
            jax.ShapeDtypeStruct((tall, channels), bf16),
            jax.ShapeDtypeStruct((patches, channels), bf16),
            jax.ShapeDtypeStruct((bins, up.shape[1]), f32),
            jax.ShapeDtypeStruct((bins, LANES), f32),
            jax.ShapeDtypeStruct((count, bins, LANES), bf16),
        ],
        in_specs=[vmem] * 8, out_specs=[vmem] * 5,
        scratch_shapes=[
            pltpu.VMEM((channels // LANES, tall, LANES), f32),
            pltpu.VMEM((2, chunk, taps.shape[0]), bf16),
            pltpu.VMEM((bins, channels), f32),
        ],
        compiler_params=pltpu.CompilerParams(vmem_limit_bytes=40 << 20),
        cost_estimate=pl.CostEstimate(flops=6_200_000_000, bytes_accessed=14_000_000, transcendentals=800_000),
        name="forward",
    )(tokens, ends, stem, taps, bias, up, gain, pair)

def input_kernel(chunk, slope, d_pooled, ends, taps, out, cells, shifted):
    patches, channels = slope.shape
    blocks = channels // LANES
    kernel = taps.shape[0] // channels
    reach = (kernel - 1) // 2
    for c in range(blocks):
        at = slice(c * LANES, (c + 1) * LANES)
        cells[c, :PAD, :] = ends[:PAD, at].astype(f32)
        cells[c, PAD + patches:, :] = ends[PAD:, at].astype(f32)
        for n in range(patches // POOL):
            rows = slice(n * POOL, (n + 1) * POOL)
            cells[c, PAD + n * POOL:PAD + (n + 1) * POOL, :] = slope[rows, at].astype(f32) * d_pooled[n:n + 1, at]
    for r in range(patches // chunk):
        total = None
        for k in range(kernel):
            for c in range(blocks):
                start = r * chunk + PAD + reach - k
                j = c * LANES
                shifted[(r * kernel + k) % 2, :, j:j + LANES] = cells[c, start:start + chunk, :].astype(bf16)
            term = lax.dot_general(shifted[(r * kernel + k) % 2], taps[k * channels:(k + 1) * channels, :], NT, preferred_element_type=f32)
            total = term if total is None else total + term
        out[r * chunk:(r + 1) * chunk, :] = total.astype(bf16)

def input_stage(slope, d_pooled, ends, taps, chunk=256):
    vmem = pl.BlockSpec(memory_space=pltpu.VMEM)
    patches, channels = slope.shape
    tall = patches + 2 * PAD
    return pl.pallas_call(
        functools.partial(input_kernel, chunk),
        out_shape=jax.ShapeDtypeStruct((patches, channels), bf16),
        in_specs=[vmem] * 4, out_specs=vmem,
        scratch_shapes=[
            pltpu.VMEM((channels // LANES, tall, LANES), f32),
            pltpu.VMEM((2, chunk, channels), bf16),
        ],
        compiler_params=pltpu.CompilerParams(vmem_limit_bytes=40 << 20),
        cost_estimate=pl.CostEstimate(flops=6_200_000_000, bytes_accessed=10_000_000, transcendentals=0),
        name="input",
    )(slope, d_pooled, ends, taps)

def tail_kernel(received, along, turned, hidden_up, inverse, kept, projection, slope, d_pooled, sketch, edges):
    patches, channels = slope.shape
    grads = jnp.sum(received[...], axis=0)[:, :2 * OP]
    inner = jnp.sum(grads * along[...], axis=1, keepdims=True)
    scale = inverse[:, :1]
    both = jnp.dot(grads, turned[...], precision=highest, preferred_element_type=f32)
    scaled = (scale * both - scale * scale * scale * inner * hidden_up[...]) * (1.0 / POOL)
    d_pooled[...] = scaled
    bins = kept.shape[0]
    total = scaled[0:1] * kept[0]
    for n in range(1, bins):
        total = total + scaled[n:n + 1] * kept[n]
    part = jnp.dot(total, projection[...], precision=highest, preferred_element_type=f32)
    sketch[...] = jnp.broadcast_to(part[None], sketch.shape)
    edges[:PAD, :] = (scaled[:1] * slope[:PAD, :].astype(f32)).astype(bf16)
    edges[PAD:, :] = (scaled[bins - 1:] * slope[patches - PAD:, :].astype(f32)).astype(bf16)


def tail_stage(received, along, turned, hidden_up, inverse, kept, projection, slope, fan):
    vmem = pl.BlockSpec(memory_space=pltpu.VMEM)
    bins, channels = hidden_up.shape
    return pl.pallas_call(
        tail_kernel,
        out_shape=[
            jax.ShapeDtypeStruct((bins, channels), f32),
            jax.ShapeDtypeStruct((fan, kept.shape[1], projection.shape[1]), f32),
            jax.ShapeDtypeStruct((2 * PAD, channels), bf16),
        ],
        in_specs=[vmem] * 8,
        out_specs=[vmem] * 3,
        compiler_params=pltpu.CompilerParams(vmem_limit_bytes=24 << 20),
        cost_estimate=pl.CostEstimate(flops=20_000_000, bytes_accessed=4_000_000, transcendentals=0),
        name="tail",
    )(received, along, turned, hidden_up, inverse, kept, projection, slope)


def to_neighbours(head, tail, axes):
    count = lax.axis_size(axes)
    ends = count - 1
    before = lax.ppermute(tail, axes, [(i, i + 1) for i in range(ends)])
    behind = lax.ppermute(head, axes, [(i + 1, i) for i in range(ends)])
    return before, behind


def one_hot(bases):
    return (
        (bases[:, :, None] == jnp.arange(4, dtype=jnp.int32))
        .astype(bf16)
        .reshape(bases.shape[0], PATCH * 4)
    )


def shards(
    tokens,
    stem_weight,
    conv_weight,
    conv_bias,
    up_weight,
    norm_gain,
    pair_weight,
    out_weight,
    cotangent,
    projection,
    buckets,
):
    channels = conv_weight.shape[1]
    wide_channels = up_weight.shape[1]
    kernel = conv_weight.shape[0] // channels
    reach = (kernel - 1) // 2
    patches = tokens.shape[1] // PATCH
    bins = patches // POOL
    line = ("seq", "col")
    count = lax.axis_size(line)
    where = jnp.stack([lax.axis_index("seq"), lax.axis_index("col")]).astype(jnp.int32)

    edge = reach * PATCH
    ahead, behind = to_neighbours(
        one_hot(tokens[0, :edge].reshape(reach, PATCH)),
        one_hot(tokens[0, -edge:].reshape(reach, PATCH)),
        line,
    )
    spread_ends = jnp.pad(jnp.concatenate([ahead, behind], axis=0), ((PAD - reach, PAD - reach), (0, 0)))
    padded, slope, hidden, inverse, parts = forward_stage(
        tokens[0].reshape(-1, LANES),
        spread_ends,
        stem_weight,
        conv_weight,
        conv_bias[None],
        up_weight,
        norm_gain[None],
        pair_weight.T,
        count,
    )
    parts = lax.all_to_all(parts, line, 0, 0, tiled=True)
    member = (
        buckets.reshape(kernel, 1, channels)
        == jnp.arange(BUCKETS, dtype=jnp.int32)[None, :, None]
    ).astype(bf16)
    tapped = lax.dot_general(
        member.reshape(kernel * BUCKETS, channels), padded, NT, preferred_element_type=f32
    )
    mixed = sum(
        tapped[k * BUCKETS : (k + 1) * BUCKETS, PAD - reach + k : PAD - reach + k + patches]
        for k in range(kernel)
    )
    mixed_hi, mixed_lo = split(mixed)
    mixed_both = jnp.concatenate([mixed_hi, mixed_lo], axis=0).reshape(2 * BUCKETS, bins, POOL)
    slopes = slope.reshape(bins, POOL, channels)
    kept = jnp.einsum("mnt,nto->nmo", mixed_both, slopes, preferred_element_type=f32)
    kept = kept[:, :BUCKETS] + kept[:, BUCKETS:]

    scaled_pair = pair_weight.astype(f32).T * norm_gain
    through = lax.dot_general(
        jnp.concatenate([split_rows(scaled_pair), split_rows(hidden)], axis=0),
        up_weight,
        NT,
        preferred_element_type=f32,
    )
    turned = through[: 2 * OP] + through[2 * OP : 4 * OP]
    hidden_up = through[4 * OP : 4 * OP + bins] + through[4 * OP + bins :]
    along = lax.dot_general(hidden, scaled_pair, NT, precision=highest)
    wide = out_weight.reshape(OP, OP * out_weight.shape[1])

    sent = pair_stage(where, parts, cotangent[0], wide)
    received = lax.all_to_all(sent, line, 0, 0, tiled=True)
    d_pooled, sketch, edges = tail_stage(
        received, along / wide_channels, turned, hidden_up, inverse, kept, projection, slope,
        lax.axis_size("seq"),
    )
    sketch = jnp.sum(lax.all_to_all(sketch, "seq", 0, 0, tiled=True), axis=0)
    col_count = lax.axis_size("col")
    batches = lax.axis_size("batch")
    every = lax.all_to_all(
        jnp.broadcast_to(sketch[None], (batches * col_count,) + sketch.shape),
        ("batch", "col"),
        0,
        0,
        tiled=True,
    )
    sketches = jnp.sum(every.reshape(batches, col_count, *sketch.shape), axis=1)
    units = sketches * lax.rsqrt(
        jnp.mean(sketches * sketches, axis=(1, 2), keepdims=True) + 1e-06
    )
    own = lax.dynamic_slice_in_dim(units, lax.axis_index("batch"), 1, 0)
    embedding = own - jnp.sum(units, axis=0, keepdims=True) / batches

    ahead, behind = to_neighbours(edges[:reach], edges[-reach:], line)
    grad_ends = jnp.pad(jnp.concatenate([ahead, behind], axis=0), ((PAD - reach, PAD - reach), (0, 0)))
    input_grad = input_stage(slope, d_pooled, grad_ends, conv_weight)
    return (input_grad[None], embedding)


def solution(mesh):
    in_specs = (
        P("batch", ("seq", "col")),
        P(),
        P(),
        P(),
        P(),
        P(),
        P(),
        P(),
        P("batch", "seq", "col", None),
        P(),
        P(),
    )
    out_specs = (P("batch", ("seq", "col"), None), P("batch", None, None))
    return jax.shard_map(shards, mesh=mesh, in_specs=in_specs, out_specs=out_specs, check_vma=False)
```

```python
import functools
import jax
import jax.numpy as jnp
from jax import lax
from jax.experimental import pallas as pl
from jax.experimental.pallas import tpu as pltpu
from jax.sharding import PartitionSpec as P


OP = 32
PATCH = 16
POOL = 128
BUCKETS = 32
LANES = 128
PAD = 8
ROOT = 0.7978845608028654
CUBIC = 0.044715

f32 = jnp.float32
bf16 = jnp.bfloat16
NT = (((1,), (1,)), ((), ()))
highest = lax.Precision.HIGHEST
HBM = pl.BlockSpec(memory_space=pl.ANY)
FULL = 67_000_000
MOST = 60 * 1024 * 1024


def split_in_kernel(x):
    hi = x.astype(bf16)
    return hi, (x - hi.astype(f32)).astype(bf16)


def pair_kernel(where, parts, cot, wide, out, moved):
    rows, cols, _ = cot.shape
    bins = parts.shape[1]
    seq, col = where[0], where[1]
    mine = parts[pl.ds(seq * (rows // bins), rows // bins)].astype(f32).reshape(rows, LANES)
    left = mine[:, :OP].astype(bf16)
    other = parts[pl.ds(col * (cols // bins), cols // bins)].astype(f32).reshape(cols, LANES)
    right = other.T[OP : 2 * OP].astype(bf16)
    grid = jnp.concatenate([cot[i] for i in range(rows)], axis=1)
    weighted = jnp.dot(left, wide[...], preferred_element_type=f32)
    for l in range(OP):
        moved[pl.ds(l, rows, stride=OP), :] = weighted[:, l * LANES : (l + 1) * LANES]
    stacked = jnp.concatenate([moved[i * OP : (i + 1) * OP, :] for i in range(rows)], axis=1)
    hi, lo = split_in_kernel(stacked)
    both = lax.dot_general(
        grid, jnp.concatenate([hi, lo], axis=0), NT, preferred_element_type=f32
    )
    grad_right = both[:, :OP] + both[:, OP:]
    summed = jnp.dot(right, grid, preferred_element_type=f32)
    for i in range(rows):
        moved[i * OP : (i + 1) * OP, :] = summed[:, i * LANES : (i + 1) * LANES]
    by_row = jnp.concatenate([moved[pl.ds(l, rows, stride=OP), :] for l in range(OP)], axis=1)
    hi, lo = split_in_kernel(by_row)
    both = lax.dot_general(
        jnp.concatenate([hi, lo], axis=0), wide[...], NT, preferred_element_type=f32
    )
    grad_left = both[:rows] + both[rows:]
    out[...] = jnp.zeros_like(out)
    out[pl.ds(seq * (rows // bins), rows // bins), :, :OP] = grad_left.reshape(-1, bins, OP)
    out[pl.ds(col * (cols // bins), cols // bins), :, OP : 2 * OP] = grad_right.reshape(
        -1, bins, OP
    )


def pair_stage(where, parts, cot, wide):
    vmem = pl.BlockSpec(memory_space=pltpu.VMEM)
    return pl.pallas_call(
        pair_kernel,
        out_shape=jax.ShapeDtypeStruct(parts.shape, f32),
        in_specs=[pl.BlockSpec(memory_space=pltpu.SMEM), vmem, vmem, vmem],
        out_specs=vmem,
        scratch_shapes=[pltpu.VMEM((cot.shape[0] * OP, LANES), f32)],
        compiler_params=pltpu.CompilerParams(vmem_limit_bytes=32 << 20),
        cost_estimate=pl.CostEstimate(flops=200_000_000, bytes_accessed=2_000_000, transcendentals=0),
        name="pair",
    )(where, parts, cot, wide)


def iota(shape, dim): return lax.broadcasted_iota(jnp.int32, shape, dim)


def forward_kernel(chunk, *refs):
    sources = refs[:8]
    spread, slope, parts, hidden_out, inverse_out, rim = refs[8:14]
    tokens, ends, stem, taps, bias, up, gain, pair = refs[14:22]
    cells, unfolded, pools, spread_here, slope_here, parts_here, sems = refs[22:]
    copies = [
        pltpu.make_async_copy(source, here, sems.at[j])
        for j, (source, here) in enumerate(zip(sources, refs[14:22]))
    ]
    for copy in copies:
        copy.start()
    patches = slope.shape[0]
    per = LANES // PATCH
    channels = stem.shape[1]
    blocks = channels // LANES
    kernel = taps.shape[0] // channels
    reach = (kernel - 1) // 2
    t = iota((patches, LANES), 0)
    lane = iota((patches, LANES), 1)
    repeat = (t // per == lane).astype(bf16)
    fold = (iota((LANES, 4 * PATCH), 0) % PATCH == iota((LANES, 4 * PATCH), 1) // 4).astype(bf16)
    copies[0].wait()
    bases = tokens[...].astype(f32).astype(bf16)
    rows = jnp.dot(repeat, bases, preferred_element_type=f32)
    own = jnp.where(lane // PATCH == t % per, rows + 1.0, 0.0).astype(bf16)
    base = jnp.dot(own, fold, preferred_element_type=f32)
    onehot = (base == (iota((patches, 4 * PATCH), 1) % 4 + 1).astype(f32)).astype(f32).astype(bf16)
    copies[1].wait()
    copies[2].wait()
    main = jnp.dot(onehot, stem[...], preferred_element_type=f32).astype(bf16)
    edges = jnp.dot(ends[...], stem[...], preferred_element_type=f32).astype(bf16)
    spread_here[:PAD, :] = edges[:PAD]
    spread_here[PAD : PAD + patches, :] = main
    spread_here[PAD + patches :, :] = edges[PAD:]
    wide = main.astype(f32)
    edges = edges.astype(f32)
    for c in range(blocks):
        at = slice(c * LANES, (c + 1) * LANES)
        cells[c, :PAD, :] = edges[:PAD, at]
        cells[c, PAD : PAD + patches, :] = wide[:, at]
        cells[c, PAD + patches :, :] = edges[PAD:, at]
    outs = [pltpu.make_async_copy(spread_here, spread, sems.at[8])]
    outs[0].start()
    for r in range(patches // chunk):
        for k in range(kernel):
            for c in range(blocks):
                start = r * chunk + PAD - reach + k
                j = (k * blocks + c) * LANES
                unfolded[r % 2, :, j : j + LANES] = cells[c, start : start + chunk, :].astype(bf16)
        if r == 0:
            copies[3].wait()
            copies[4].wait()
        before = jnp.dot(unfolded[r % 2], taps[...], preferred_element_type=f32) + bias[...]
        square = before * before
        bent = jnp.tanh(before * (ROOT + ROOT * CUBIC * square))
        half = 0.5 * (1.0 + bent)
        after = before * half
        tilt = half + before * (0.5 - 0.5 * bent * bent) * (ROOT + 3.0 * ROOT * CUBIC * square)
        slope_here[r * chunk : (r + 1) * chunk, :] = tilt.astype(bf16)
        out = pltpu.make_async_copy(
            slope_here.at[pl.ds(r * chunk, chunk)], slope.at[pl.ds(r * chunk, chunk)], sems.at[10 + r]
        )
        out.start()
        outs.append(out)
        for n in range(chunk // POOL):
            b = r * (chunk // POOL) + n
            pools[b : b + 1, :] = jnp.sum(
                after[n * POOL : (n + 1) * POOL], axis=0, keepdims=True
            ) * (1.0 / POOL)
    rim[:PAD, :] = slope_here[:PAD, :]
    rim[PAD:, :] = slope_here[patches - PAD :, :]
    for copy in copies[5:]:
        copy.wait()
    hidden = jnp.dot(pools[...].astype(bf16), up[...], preferred_element_type=f32)
    inverse = lax.rsqrt(jnp.mean(hidden * hidden, axis=1, keepdims=True) + 1e-06)
    normed = (hidden * inverse * gain[...]).astype(bf16)
    sides = lax.dot_general(normed, pair[...], NT, preferred_element_type=f32)
    full = jnp.concatenate([sides, jnp.zeros_like(sides)], axis=1).astype(bf16)
    parts_here[...] = jnp.broadcast_to(full[None], parts.shape)
    out = pltpu.make_async_copy(parts_here, parts, sems.at[9])
    out.start()
    outs.append(out)
    hidden_out[...] = hidden
    inverse_out[...] = jnp.broadcast_to(inverse, inverse_out.shape)
    for out in outs:
        out.wait()


def forward_stage(tokens, ends, stem, taps, bias, up, gain, pair, count, chunk=512):
    vmem = pl.BlockSpec(memory_space=pltpu.VMEM)
    patches = tokens.size // PATCH
    channels = stem.shape[1]
    bins = patches // POOL
    tall = patches + 2 * PAD
    inputs = (tokens, ends, stem, taps, bias, up, gain, pair)
    return pl.pallas_call(
        functools.partial(forward_kernel, chunk),
        out_shape=[
            jax.ShapeDtypeStruct((tall, channels), bf16),
            jax.ShapeDtypeStruct((patches, channels), bf16),
            jax.ShapeDtypeStruct((count, bins, LANES), bf16),
            jax.ShapeDtypeStruct((bins, up.shape[1]), f32),
            jax.ShapeDtypeStruct((bins, LANES), f32),
            jax.ShapeDtypeStruct((2 * PAD, channels), bf16),
        ],
        in_specs=[HBM] * 8,
        out_specs=[HBM] * 3 + [vmem] * 3,
        scratch_shapes=[pltpu.VMEM(x.shape, x.dtype) for x in inputs]
        + [
            pltpu.VMEM((channels // LANES, tall, LANES), f32),
            pltpu.VMEM((2, chunk, taps.shape[0]), bf16),
            pltpu.VMEM((bins, channels), f32),
            pltpu.VMEM((tall, channels), bf16),
            pltpu.VMEM((patches, channels), bf16),
            pltpu.VMEM((count, bins, LANES), bf16),
            pltpu.SemaphoreType.DMA((10 + patches // chunk,)),
        ],
        compiler_params=pltpu.CompilerParams(vmem_limit_bytes=FULL),
        cost_estimate=pl.CostEstimate(
            flops=6_200_000_000, bytes_accessed=14_000_000, transcendentals=800_000
        ),
        name="forward",
    )(*inputs)


def input_rows(segments, fills, source, d_pooled, ends, taps, out, cells, shifted, taps_here, block, slope, sems):
    patches, channels = slope.shape
    first = pltpu.make_async_copy(source, slope, sems.at[sems.shape[0] - 1])
    first.start()
    blocks = channels // LANES
    kernel = taps.shape[0] // channels
    reach = (kernel - 1) // 2
    copies = [
        pltpu.make_async_copy(
            taps.at[pl.ds(k * channels, channels)],
            taps_here.at[pl.ds(k * channels, channels)],
            sems.at[k],
        )
        for k in range(kernel)
    ]
    for copy in copies:
        copy.start()
    first.wait()
    for c in range(blocks):
        at = slice(c * LANES, (c + 1) * LANES)
        if ends is not None:
            cells[c, :PAD, :] = ends[:PAD, at].astype(f32)
            cells[c, PAD + patches :, :] = ends[PAD:, at].astype(f32)
        for low, high in fills:
            n = low // POOL
            cells[c, PAD + low : PAD + high, :] = (
                slope[low:high, at].astype(f32) * d_pooled[n : n + 1, at]
            )
    total = None
    for k in range(kernel):
        at = 0
        for low, rows in segments:
            start = low + PAD + reach - k
            for c in range(blocks):
                shifted[k % 2, at : at + rows, c * LANES : (c + 1) * LANES] = cells[
                    c, start : start + rows, :
                ].astype(bf16)
            at += rows
        copies[k].wait()
        term = lax.dot_general(
            shifted[k % 2],
            taps_here[k * channels : (k + 1) * channels, :],
            NT,
            preferred_element_type=f32,
        )
        total = term if total is None else total + term
    block[...] = total.astype(bf16)
    at = 0
    backs = []
    for j, (low, rows) in enumerate(segments):
        backs.append(
            pltpu.make_async_copy(
                block.at[pl.ds(at, rows)], out.at[pl.ds(low, rows)], sems.at[kernel + j]
            )
        )
        at += rows
    for back in backs:
        back.start()
    for back in backs:
        back.wait()


def inner_kernel(segments, fills, slope, d_pooled, taps, out, *scratch):
    input_rows(segments, fills, slope, d_pooled, None, taps, out, *scratch)


def outer_kernel(segments, fills, slope, d_pooled, ends, taps, partial, out, *scratch):
    input_rows(segments, fills, slope, d_pooled, ends, taps, out, *scratch)


def input_scratch(rows, slope, taps):
    patches, channels = slope.shape
    kernel = taps.shape[0] // channels
    return [
        pltpu.VMEM((channels // LANES, patches + 2 * PAD, LANES), f32),
        pltpu.VMEM((2, rows, channels), bf16),
        pltpu.VMEM(taps.shape, bf16),
        pltpu.VMEM((rows, channels), bf16),
        pltpu.VMEM(slope.shape, bf16),
        pltpu.SemaphoreType.DMA((kernel + 3,)),
    ]


def inner_stage(slope, d_pooled, taps):
    vmem = pl.BlockSpec(memory_space=pltpu.VMEM)
    patches, channels = slope.shape
    bins = patches // POOL
    rows = patches - 2 * POOL
    fills = [(POOL - 16, POOL)]
    fills += [(n * POOL, (n + 1) * POOL) for n in range(1, bins - 1)]
    fills += [(patches - POOL, patches - POOL + 16)]
    return pl.pallas_call(
        functools.partial(inner_kernel, [(POOL, rows)], fills),
        out_shape=jax.ShapeDtypeStruct((patches, channels), bf16),
        in_specs=[HBM, vmem, HBM],
        out_specs=HBM,
        scratch_shapes=input_scratch(rows, slope, taps),
        compiler_params=pltpu.CompilerParams(vmem_limit_bytes=MOST),
        cost_estimate=pl.CostEstimate(
            flops=4_600_000_000, bytes_accessed=9_000_000, transcendentals=0
        ),
        name="inner",
    )(slope, d_pooled, taps)


def outer_stage(slope, d_pooled, ends, taps, partial):
    vmem = pl.BlockSpec(memory_space=pltpu.VMEM)
    patches, channels = slope.shape
    far = patches - POOL
    fills = [(0, POOL), (POOL, POOL + 16), (far - 16, far), (far, patches)]
    return pl.pallas_call(
        functools.partial(outer_kernel, [(0, POOL), (far, POOL)], fills),
        out_shape=jax.ShapeDtypeStruct((patches, channels), bf16),
        in_specs=[HBM, vmem, vmem, HBM, HBM],
        out_specs=HBM,
        scratch_shapes=input_scratch(2 * POOL, slope, taps),
        input_output_aliases={4: 0},
        compiler_params=pltpu.CompilerParams(vmem_limit_bytes=MOST),
        cost_estimate=pl.CostEstimate(
            flops=1_600_000_000, bytes_accessed=7_000_000, transcendentals=0
        ),
        name="outer",
    )(slope, d_pooled, ends, taps, partial)


def weights_kernel(hidden, pair, gain, up, turned, hidden_up, along, up_here, sems):
    _, wide = up.shape
    bins = hidden.shape[0]
    part = up_here.shape[0] // sems.shape[0]
    copies = [
        pltpu.make_async_copy(
            up.at[pl.ds(j * part, part)], up_here.at[pl.ds(j * part, part)], sems.at[j]
        )
        for j in range(sems.shape[0])
    ]
    for copy in copies:
        copy.start()
    scaled = pair[...].astype(f32) * gain[...]
    along[...] = lax.dot_general(
        hidden[...], scaled, NT, precision=highest, preferred_element_type=f32
    ) * (1.0 / wide)
    scaled_hi, scaled_lo = split_in_kernel(scaled)
    hidden_hi, hidden_lo = split_in_kernel(hidden[...])
    stacked = jnp.concatenate(
        [scaled_hi.astype(f32), scaled_lo.astype(f32), hidden_hi.astype(f32), hidden_lo.astype(f32)],
        axis=0,
    ).astype(bf16)
    for j, copy in enumerate(copies):
        copy.wait()
        at = slice(j * part, (j + 1) * part)
        through = lax.dot_general(stacked, up_here[at, :], NT, preferred_element_type=f32)
        turned[:, at] = through[: 2 * OP] + through[2 * OP : 4 * OP]
        hidden_up[:, at] = through[4 * OP : 4 * OP + bins] + through[4 * OP + bins :]


def weights_stage(hidden, pair, gain, up):
    vmem = pl.BlockSpec(memory_space=pltpu.VMEM)
    bins, _ = hidden.shape
    channels = up.shape[0]
    return pl.pallas_call(
        weights_kernel,
        out_shape=[
            jax.ShapeDtypeStruct((2 * OP, channels), f32),
            jax.ShapeDtypeStruct((bins, channels), f32),
            jax.ShapeDtypeStruct((bins, 2 * OP), f32),
        ],
        in_specs=[vmem, vmem, vmem, HBM],
        out_specs=[vmem] * 3,
        scratch_shapes=[pltpu.VMEM(up.shape, bf16), pltpu.SemaphoreType.DMA((3,))],
        compiler_params=pltpu.CompilerParams(vmem_limit_bytes=16 << 20),
        cost_estimate=pl.CostEstimate(
            flops=340_000_000, bytes_accessed=3_000_000, transcendentals=0
        ),
        name="weights",
    )(hidden, pair, gain, up)


def bins_kernel(buckets, spread, slope, kept):
    kernel, channels = buckets.shape
    patches = slope.shape[0]
    reach = (kernel - 1) // 2
    slots = iota((BUCKETS, channels), 0)
    member = jnp.concatenate(
        [(buckets[k : k + 1, :] == slots).astype(f32) for k in range(kernel)], axis=0
    ).astype(bf16)
    tapped = lax.dot_general(member, spread[...], NT, preferred_element_type=f32)
    mixed = None
    for k in range(kernel):
        start = PAD - reach + k
        term = tapped[k * BUCKETS : (k + 1) * BUCKETS, start : start + patches]
        mixed = term if mixed is None else mixed + term
    hi, lo = split_in_kernel(mixed)
    both = jnp.concatenate([hi, lo], axis=0)
    for n in range(patches // POOL):
        rows = slice(n * POOL, (n + 1) * POOL)
        part = jnp.dot(both[:, rows], slope[rows, :], preferred_element_type=f32)
        kept[n] = part[:BUCKETS] + part[BUCKETS:]


def bins_stage(buckets, spread, slope):
    vmem = pl.BlockSpec(memory_space=pltpu.VMEM)
    patches, channels = slope.shape
    return pl.pallas_call(
        bins_kernel,
        out_shape=jax.ShapeDtypeStruct((patches // POOL, BUCKETS, channels), f32),
        in_specs=[vmem] * 3,
        out_specs=vmem,
        compiler_params=pltpu.CompilerParams(vmem_limit_bytes=24 << 20),
        cost_estimate=pl.CostEstimate(
            flops=400_000_000, bytes_accessed=4_000_000, transcendentals=0
        ),
        name="bins",
    )(buckets, spread, slope)


def tail_kernel(received, along, turned, hidden_up, inverse, kept, projection, rim, d_pooled, sketch, edges):
    grads = jnp.sum(received[...], axis=0)[:, :2 * OP]
    inner = jnp.sum(grads * along[...], axis=1, keepdims=True)
    scale = inverse[:, :1]
    both = jnp.dot(grads, turned[...], precision=highest, preferred_element_type=f32)
    scaled = (scale * both - scale * scale * scale * inner * hidden_up[...]) * (1.0 / POOL)
    d_pooled[...] = scaled
    bins = kept.shape[0]
    total = scaled[0:1] * kept[0]
    for n in range(1, bins):
        total = total + scaled[n:n + 1] * kept[n]
    part = jnp.dot(total, projection[...], precision=highest, preferred_element_type=f32)
    sketch[...] = jnp.broadcast_to(part[None], sketch.shape)
    edges[:PAD, :] = (scaled[:1] * rim[:PAD, :].astype(f32)).astype(bf16)
    edges[PAD:, :] = (scaled[bins - 1:] * rim[PAD:, :].astype(f32)).astype(bf16)


def tail_stage(received, along, turned, hidden_up, inverse, kept, projection, rim, fan):
    vmem = pl.BlockSpec(memory_space=pltpu.VMEM)
    bins, channels = hidden_up.shape
    return pl.pallas_call(
        tail_kernel,
        out_shape=[
            jax.ShapeDtypeStruct((bins, channels), f32),
            jax.ShapeDtypeStruct((fan, kept.shape[1], projection.shape[1]), f32),
            jax.ShapeDtypeStruct((2 * PAD, channels), bf16),
        ],
        in_specs=[vmem] * 8,
        out_specs=[vmem] * 3,
        compiler_params=pltpu.CompilerParams(vmem_limit_bytes=24 << 20),
        cost_estimate=pl.CostEstimate(flops=20_000_000, bytes_accessed=4_000_000, transcendentals=0),
        name="tail",
    )(received, along, turned, hidden_up, inverse, kept, projection, rim)


def to_neighbours(head, tail, axes):
    count = lax.axis_size(axes)
    place = lax.axis_index(axes)
    even = place % 2 == 0
    inside = [(i, i ^ 1) for i in range(count)]
    across = [(0, 0), (count - 1, count - 1)] + [
        (i, i + 1 if i % 2 else i - 1) for i in range(1, count - 1)
    ]
    far = lax.ppermute(jnp.where(even, head, tail), axes, across)
    near = lax.ppermute(jnp.where(even, tail, head), axes, inside)
    before = jnp.where(even, far, near)
    behind = jnp.where(even, near, far)
    before = jnp.where(place > 0, before, jnp.zeros_like(before))
    behind = jnp.where(place < count - 1, behind, jnp.zeros_like(behind))
    reach = head.shape[0]
    return jnp.pad(
        jnp.concatenate([before, behind], axis=0), ((PAD - reach, PAD - reach), (0, 0))
    )


def one_hot(bases):
    return (
        (bases[:, :, None] == jnp.arange(4, dtype=jnp.int32))
        .astype(bf16)
        .reshape(bases.shape[0], PATCH * 4)
    )


def exchange(value, axes):
    return lax.all_to_all(value, axes, 0, 0, tiled=True)


def whole(
    tokens,
    stem_weight,
    conv_weight,
    conv_bias,
    up_weight,
    norm_gain,
    pair_weight,
    out_weight,
    cotangent,
    projection,
    buckets,
):
    channels = conv_weight.shape[1]
    kernel = conv_weight.shape[0] // channels
    reach = (kernel - 1) // 2
    line = ("seq", "col")
    count = lax.axis_size(line)
    where = jnp.stack([lax.axis_index("seq"), lax.axis_index("col")]).astype(jnp.int32)

    edge = reach * PATCH
    ends = to_neighbours(
        one_hot(tokens[0, :edge].reshape(reach, PATCH)),
        one_hot(tokens[0, -edge:].reshape(reach, PATCH)),
        line,
    )
    pair = pair_weight.T
    gain = norm_gain[None]
    spread, slope, parts, hidden, inverse, rim = forward_stage(
        tokens[0].reshape(-1, LANES), ends, stem_weight, conv_weight, conv_bias[None], up_weight,
        gain, pair, count,
    )
    parts = exchange(parts, line)
    turned, hidden_up, along = weights_stage(hidden, pair, gain, up_weight)
    wide = out_weight.reshape(OP, OP * out_weight.shape[1])
    sent = pair_stage(where, parts, cotangent[0], wide)
    received = exchange(sent, line)
    kept = bins_stage(buckets.reshape(kernel, channels), spread, slope)
    d_pooled, sketch, edges = tail_stage(
        received, along, turned, hidden_up, inverse, kept, projection, rim,
        lax.axis_size("seq"),
    )
    sketch = jnp.sum(exchange(sketch, "seq"), axis=0)
    partial = inner_stage(slope, d_pooled, conv_weight)
    grad_ends = to_neighbours(edges[:reach], edges[-reach:], line)
    col_count = lax.axis_size("col")
    batches = lax.axis_size("batch")
    every = exchange(
        jnp.broadcast_to(sketch[None], (batches * col_count,) + sketch.shape), ("batch", "col")
    )
    input_grad = outer_stage(slope, d_pooled, grad_ends, conv_weight, partial)
    sketches = jnp.sum(every.reshape(batches, col_count, *sketch.shape), axis=1)
    units = sketches * lax.rsqrt(
        jnp.mean(sketches * sketches, axis=(1, 2), keepdims=True) + 1e-06
    )
    own = lax.dynamic_slice_in_dim(units, lax.axis_index("batch"), 1, 0)
    embedding = own - jnp.sum(units, axis=0, keepdims=True) / batches
    return (input_grad[None], embedding)


def solution(mesh):
    in_specs = (
        P("batch", ("seq", "col")),
        P(),
        P(),
        P(),
        P(),
        P(),
        P(),
        P(),
        P("batch", "seq", "col", None),
        P(),
        P(),
    )
    out_specs = (P("batch", ("seq", "col"), None), P("batch", None, None))
    return jax.shard_map(whole, mesh=mesh, in_specs=in_specs, out_specs=out_specs, check_vma=False)
```

```python
import functools
import jax
import jax.numpy as jnp
from jax import lax
from jax.experimental import pallas as pl
from jax.experimental.pallas import tpu as pltpu
from jax.sharding import PartitionSpec as P


OP = 32
PATCH = 16
POOL = 128
BUCKETS = 32
LANES = 128
PAD = 8
ROOT = 0.7978845608028654
CUBIC = 0.044715

f32 = jnp.float32
bf16 = jnp.bfloat16
NT = (((1,), (1,)), ((), ()))
highest = lax.Precision.HIGHEST
HBM = pl.BlockSpec(memory_space=pl.ANY)
FULL = 67_000_000
MOST = 60 * 1024 * 1024


def split_in_kernel(x):
    hi = x.astype(bf16)
    return hi, (x - hi.astype(f32)).astype(bf16)


def pair_kernel(where, parts_in, cot_in, wide_in, out, moved, placed, parts, cot, wide, sems):
    copies = [
        pltpu.make_async_copy(source, here, sems.at[j])
        for j, (source, here) in enumerate(((parts_in, parts), (wide_in, wide), (cot_in, cot)))
    ]
    for copy in copies:
        copy.start()
    for copy in copies[:2]:
        copy.wait()
    rows, cols, _ = cot.shape
    bins = parts.shape[1]
    seq, col = where[0], where[1]
    mine = parts[pl.ds(seq * (rows // bins), rows // bins)].astype(f32).reshape(rows, LANES)
    left = mine[:, :OP].astype(bf16)
    other = parts[pl.ds(col * (cols // bins), cols // bins)].astype(f32).reshape(cols, LANES)
    right = other.T[OP : 2 * OP].astype(bf16)
    weighted = jnp.dot(left, wide[...], preferred_element_type=f32)
    for l in range(OP):
        moved[pl.ds(l, rows, stride=OP), :] = weighted[:, l * LANES : (l + 1) * LANES]
    copies[2].wait()
    grid = jnp.concatenate([cot[i] for i in range(rows)], axis=1)
    stacked = jnp.concatenate([moved[i * OP : (i + 1) * OP, :] for i in range(rows)], axis=1)
    hi, lo = split_in_kernel(stacked)
    both = lax.dot_general(
        grid, jnp.concatenate([hi, lo], axis=0), NT, preferred_element_type=f32
    )
    grad_right = both[:, :OP] + both[:, OP:]
    summed = jnp.dot(right, grid, preferred_element_type=f32)
    for i in range(rows):
        moved[i * OP : (i + 1) * OP, :] = summed[:, i * LANES : (i + 1) * LANES]
    by_row = jnp.concatenate([moved[pl.ds(l, rows, stride=OP), :] for l in range(OP)], axis=1)
    hi, lo = split_in_kernel(by_row)
    both = lax.dot_general(
        jnp.concatenate([hi, lo], axis=0), wide[...], NT, preferred_element_type=f32
    )
    grad_left = both[:rows] + both[rows:]
    placed[...] = jnp.zeros_like(placed)
    for index, grads, lane in (
        (seq * (rows // bins), grad_left, 0),
        (col * (cols // bins), grad_right, OP),
    ):
        grads = grads.reshape(-1, bins, OP)
        many = grads.shape[0]
        own = slice(lane, lane + OP)
        beside = slice(2 * OP + lane, 3 * OP + lane)
        placed[pl.ds(index + 1, many), :, own] = grads
        placed[pl.ds(index + 2, many), :1, beside] = grads[:, bins - 1 :, :]
        placed[pl.ds(index, many), bins - 1 :, beside] = grads[:, :1, :]
    out[...] = placed[1 : 1 + out.shape[0]].astype(bf16)


def pair_stage(where, parts, cot, wide):
    vmem = pl.BlockSpec(memory_space=pltpu.VMEM)
    return pl.pallas_call(
        pair_kernel,
        out_shape=jax.ShapeDtypeStruct(parts.shape, bf16),
        in_specs=[pl.BlockSpec(memory_space=pltpu.SMEM), HBM, HBM, HBM],
        out_specs=vmem,
        scratch_shapes=[
            pltpu.VMEM((cot.shape[0] * OP, LANES), f32),
            pltpu.VMEM((parts.shape[0] + 2,) + parts.shape[1:], f32),
            pltpu.VMEM(parts.shape, bf16),
            pltpu.VMEM(cot.shape, bf16),
            pltpu.VMEM(wide.shape, bf16),
            pltpu.SemaphoreType.DMA((3,)),
        ],
        compiler_params=pltpu.CompilerParams(vmem_limit_bytes=FULL),
        cost_estimate=pl.CostEstimate(flops=200_000_000, bytes_accessed=2_000_000, transcendentals=0),
        name="pair",
    )(where, parts, cot, wide)


def iota(shape, dim): return lax.broadcasted_iota(jnp.int32, shape, dim)


def from_sides(where, far, near):
    even = where[2] % 2 == 0
    before = jnp.where(even, far, near)
    behind = jnp.where(even, near, far)
    before = jnp.where(where[2] > 0, before, jnp.zeros_like(before))
    behind = jnp.where(where[2] < where[3] - 1, behind, jnp.zeros_like(behind))
    return before, behind


def forward_kernel(chunk, where, *refs):
    sources = refs[:9]
    spread, slope, parts, hidden_out, inverse_out, rim = refs[9:15]
    tokens, far, near, stem, taps, bias, up, gain, pair = refs[15:24]
    cells, unfolded, pools, spread_here, slope_here, parts_here, sems = refs[24:]
    copies = [
        pltpu.make_async_copy(source, here, sems.at[j])
        for j, (source, here) in enumerate(zip(sources, refs[15:24]))
    ]
    for copy in copies:
        copy.start()
    patches = slope.shape[0]
    per = LANES // PATCH
    channels = stem.shape[1]
    blocks = channels // LANES
    kernel = taps.shape[0] // channels
    reach = (kernel - 1) // 2
    t = iota((patches, LANES), 0)
    lane = iota((patches, LANES), 1)
    repeat = (t // per == lane).astype(bf16)
    fold = (iota((LANES, 4 * PATCH), 0) % PATCH == iota((LANES, 4 * PATCH), 1) // 4).astype(bf16)
    copies[0].wait()
    bases = tokens[...].astype(f32).astype(bf16)
    rows = jnp.dot(repeat, bases, preferred_element_type=f32)
    own = jnp.where(lane // PATCH == t % per, rows + 1.0, 0.0).astype(bf16)
    base = jnp.dot(own, fold, preferred_element_type=f32)
    onehot = (base == (iota((patches, 4 * PATCH), 1) % 4 + 1).astype(f32)).astype(f32).astype(bf16)
    for copy in copies[1:4]:
        copy.wait()
    main = jnp.dot(onehot, stem[...], preferred_element_type=f32).astype(bf16)
    before, behind = from_sides(where, far[...].astype(f32), near[...].astype(f32))
    ends = jnp.concatenate([before[:PAD], behind[PAD:]], axis=0).astype(bf16)
    edges = jnp.dot(ends, stem[...], preferred_element_type=f32).astype(bf16)
    spread_here[:PAD, :] = edges[:PAD]
    spread_here[PAD : PAD + patches, :] = main
    spread_here[PAD + patches :, :] = edges[PAD:]
    wide = main.astype(f32)
    edges = edges.astype(f32)
    for c in range(blocks):
        at = slice(c * LANES, (c + 1) * LANES)
        cells[c, :PAD, :] = edges[:PAD, at]
        cells[c, PAD : PAD + patches, :] = wide[:, at]
        cells[c, PAD + patches :, :] = edges[PAD:, at]
    outs = [pltpu.make_async_copy(spread_here, spread, sems.at[9])]
    outs[0].start()
    for r in range(patches // chunk):
        for k in range(kernel):
            for c in range(blocks):
                start = r * chunk + PAD - reach + k
                j = (k * blocks + c) * LANES
                unfolded[r % 2, :, j : j + LANES] = cells[c, start : start + chunk, :].astype(bf16)
        if r == 0:
            copies[4].wait()
            copies[5].wait()
        before = jnp.dot(unfolded[r % 2], taps[...], preferred_element_type=f32) + bias[...].reshape(1, channels)
        square = before * before
        bent = jnp.tanh(before * (ROOT + ROOT * CUBIC * square))
        half = 0.5 * (1.0 + bent)
        after = before * half
        tilt = half + before * (0.5 - 0.5 * bent * bent) * (ROOT + 3.0 * ROOT * CUBIC * square)
        slope_here[r * chunk : (r + 1) * chunk, :] = tilt.astype(bf16)
        out = pltpu.make_async_copy(
            slope_here.at[pl.ds(r * chunk, chunk)], slope.at[pl.ds(r * chunk, chunk)], sems.at[11 + r]
        )
        out.start()
        outs.append(out)
        for n in range(chunk // POOL):
            b = r * (chunk // POOL) + n
            pools[b : b + 1, :] = jnp.sum(
                after[n * POOL : (n + 1) * POOL], axis=0, keepdims=True
            ) * (1.0 / POOL)
    rim[:PAD, :] = slope_here[:PAD, :]
    rim[PAD:, :] = slope_here[patches - PAD :, :]
    for copy in copies[6:]:
        copy.wait()
    hidden = jnp.dot(pools[...].astype(bf16), up[...], preferred_element_type=f32)
    inverse = lax.rsqrt(jnp.mean(hidden * hidden, axis=1, keepdims=True) + 1e-06)
    normed = (hidden * inverse * gain[...].reshape(1, -1)).astype(bf16)
    sides = lax.dot_general(normed, pair[...], NT, preferred_element_type=f32)
    full = jnp.concatenate([sides, jnp.zeros_like(sides)], axis=1).astype(bf16)
    parts_here[...] = jnp.broadcast_to(full[None], parts.shape)
    out = pltpu.make_async_copy(parts_here, parts, sems.at[10])
    out.start()
    outs.append(out)
    hidden_out[...] = hidden
    inverse_out[...] = jnp.broadcast_to(inverse, inverse_out.shape)
    for out in outs:
        out.wait()


def forward_stage(where, tokens, far, near, stem, taps, bias, up, gain, pair, count, chunk=512):
    vmem = pl.BlockSpec(memory_space=pltpu.VMEM)
    patches = tokens.size // PATCH
    channels = stem.shape[1]
    bins = patches // POOL
    tall = patches + 2 * PAD
    inputs = (tokens, far, near, stem, taps, bias, up, gain, pair)
    return pl.pallas_call(
        functools.partial(forward_kernel, chunk),
        out_shape=[
            jax.ShapeDtypeStruct((tall, channels), bf16),
            jax.ShapeDtypeStruct((patches, channels), bf16),
            jax.ShapeDtypeStruct((count, bins, LANES), bf16),
            jax.ShapeDtypeStruct((bins, up.shape[1]), f32),
            jax.ShapeDtypeStruct((bins, LANES), f32),
            jax.ShapeDtypeStruct((2 * PAD, channels), bf16),
        ],
        in_specs=[pl.BlockSpec(memory_space=pltpu.SMEM)] + [HBM] * 9,
        out_specs=[HBM] * 3 + [vmem] * 3,
        scratch_shapes=[pltpu.VMEM(x.shape, x.dtype) for x in inputs]
        + [
            pltpu.VMEM((channels // LANES, tall, LANES), f32),
            pltpu.VMEM((2, chunk, taps.shape[0]), bf16),
            pltpu.VMEM((bins, channels), f32),
            pltpu.VMEM((tall, channels), bf16),
            pltpu.VMEM((patches, channels), bf16),
            pltpu.VMEM((count, bins, LANES), bf16),
            pltpu.SemaphoreType.DMA((11 + patches // chunk,)),
        ],
        compiler_params=pltpu.CompilerParams(vmem_limit_bytes=FULL),
        cost_estimate=pl.CostEstimate(
            flops=6_200_000_000, bytes_accessed=14_000_000, transcendentals=800_000
        ),
        name="forward",
    )(where, *inputs)


def input_kernel(chunk, source, d_pooled, ends, taps_in, out, cells, shifted, taps, slope, block, sems):
    patches, channels = slope.shape
    blocks = channels // LANES
    kernel = taps.shape[0] // channels
    reach = (kernel - 1) // 2
    halves = 1
    part = patches // halves
    reads = [
        pltpu.make_async_copy(
            source.at[pl.ds(h * part, part)], slope.at[pl.ds(h * part, part)], sems.at[h]
        )
        for h in range(halves)
    ]
    copies = [
        pltpu.make_async_copy(
            taps_in.at[pl.ds(k * channels, channels)],
            taps.at[pl.ds(k * channels, channels)],
            sems.at[halves + k],
        )
        for k in range(kernel)
    ]
    for copy in reads + copies:
        copy.start()
    for copy in reads:
        copy.wait()
    for c in range(blocks):
        at = slice(c * LANES, (c + 1) * LANES)
        cells[c, :PAD, :] = ends[:PAD, at].astype(f32)
        cells[c, PAD + patches :, :] = ends[PAD:, at].astype(f32)
        for n in range(patches // POOL):
            low, high = n * POOL, (n + 1) * POOL
            cells[c, PAD + low : PAD + high, :] = (
                slope[low:high, at].astype(f32) * d_pooled[n : n + 1, at]
            )

    def shift(r):
        for k in range(kernel):
            start = r * chunk + PAD + reach - k
            for c in range(blocks):
                j = (k * blocks + c) * LANES
                shifted[r % 2, :, j : j + LANES] = cells[c, start : start + chunk, :].astype(bf16)

    shift(0)
    for copy in copies:
        copy.wait()
    backs = []
    for r in range(patches // chunk):
        if r > 0:
            shift(r)
        total = None
        for k in range(kernel):
            at = slice(k * channels, (k + 1) * channels)
            term = lax.dot_general(
                shifted[r % 2, :, at], taps[at, :], NT, preferred_element_type=f32
            )
            total = term if total is None else total + term
        block[r * chunk : (r + 1) * chunk, :] = total.astype(bf16)
        back = pltpu.make_async_copy(
            block.at[pl.ds(r * chunk, chunk)],
            out.at[pl.ds(r * chunk, chunk)],
            sems.at[halves + kernel + r],
        )
        back.start()
        backs.append(back)
    for back in backs:
        back.wait()


def input_stage(slope, d_pooled, ends, taps, chunk=512):
    vmem = pl.BlockSpec(memory_space=pltpu.VMEM)
    patches, channels = slope.shape
    kernel = taps.shape[0] // channels
    return pl.pallas_call(
        functools.partial(input_kernel, chunk),
        out_shape=jax.ShapeDtypeStruct((patches, channels), bf16),
        in_specs=[HBM, vmem, vmem, HBM],
        out_specs=HBM,
        scratch_shapes=[
            pltpu.VMEM((channels // LANES, patches + 2 * PAD, LANES), f32),
            pltpu.VMEM((2, chunk, taps.shape[0]), bf16),
            pltpu.VMEM(taps.shape, bf16),
            pltpu.VMEM(slope.shape, bf16),
            pltpu.VMEM((patches, channels), bf16),
            pltpu.SemaphoreType.DMA((1 + kernel + patches // chunk,)),
        ],
        compiler_params=pltpu.CompilerParams(vmem_limit_bytes=MOST),
        cost_estimate=pl.CostEstimate(
            flops=6_100_000_000, bytes_accessed=10_000_000, transcendentals=0
        ),
        name="inner",
    )(slope, d_pooled, ends, taps)


def weights_kernel(*refs):
    turned, hidden_up, along, shared, wide = refs[7:12]
    hidden, inverse, rim, pair, gain, up, mixing = refs[12:19]
    moved, sems = refs[19:]
    copies = [
        pltpu.make_async_copy(source, here, sems.at[j])
        for j, (source, here) in enumerate(zip(refs[:7], refs[12:19]))
    ]
    for copy in copies:
        copy.start()
    for copy in copies:
        copy.wait()
    _, width = up.shape
    bins = hidden.shape[0]
    scaled = pair[...].astype(f32) * gain[...].reshape(1, width)
    near = lax.dot_general(
        hidden[...], scaled, NT, precision=highest, preferred_element_type=f32
    ) * (1.0 / width)
    along[...] = near
    scaled_hi, scaled_lo = split_in_kernel(scaled)
    hidden_hi, hidden_lo = split_in_kernel(hidden[...])
    stacked = jnp.concatenate(
        [scaled_hi.astype(f32), scaled_lo.astype(f32), hidden_hi.astype(f32), hidden_lo.astype(f32)],
        axis=0,
    ).astype(bf16)
    through = lax.dot_general(stacked, up[...], NT, preferred_element_type=f32)
    turned[...] = through[: 2 * OP] + through[2 * OP : 4 * OP]
    lifted = through[4 * OP : 4 * OP + bins] + through[4 * OP + bins :]
    hidden_up[...] = lifted
    shared[...] = jnp.zeros_like(shared)
    for base, bin_at, row in ((0, bins - 1, 2 * PAD - 2), (PAD, 0, 0)):
        shared[base : base + 2, :] = rim[...].astype(f32)[row : row + 2]
        shared[base + 2 : base + 3, :] = lifted[bin_at : bin_at + 1]
        shared[base + 3 : base + 4, : 2 * OP] = near[bin_at : bin_at + 1]
        shared[base + 4 : base + 5, :LANES] = inverse[bin_at : bin_at + 1, :]
    moved[...] = mixing[...].astype(f32)
    for l in range(OP):
        wide[:, l * LANES : (l + 1) * LANES] = moved[pl.ds(l, OP, stride=OP), :].astype(bf16)


def weights_stage(hidden, inverse, rim, pair, gain, up, mixing):
    vmem = pl.BlockSpec(memory_space=pltpu.VMEM)
    bins, _ = hidden.shape
    channels = up.shape[0]
    inputs = (hidden, inverse, rim, pair, gain, up, mixing)
    return pl.pallas_call(
        weights_kernel,
        out_shape=[
            jax.ShapeDtypeStruct((2 * OP, channels), f32),
            jax.ShapeDtypeStruct((bins, channels), f32),
            jax.ShapeDtypeStruct((bins, 2 * OP), f32),
            jax.ShapeDtypeStruct((2 * PAD, channels), f32),
            jax.ShapeDtypeStruct((OP, OP * LANES), bf16),
        ],
        in_specs=[HBM] * 7,
        out_specs=[vmem] * 5,
        scratch_shapes=[pltpu.VMEM(x.shape, x.dtype) for x in inputs]
        + [pltpu.VMEM(mixing.shape, f32), pltpu.SemaphoreType.DMA((7,))],
        compiler_params=pltpu.CompilerParams(vmem_limit_bytes=FULL),
        cost_estimate=pl.CostEstimate(
            flops=340_000_000, bytes_accessed=3_000_000, transcendentals=0
        ),
        name="weights",
    )(*inputs)


def bins_kernel(buckets, spread, slope, kept):
    kernel, channels = buckets.shape
    patches = slope.shape[0]
    reach = (kernel - 1) // 2
    slots = iota((BUCKETS, channels), 0)
    member = jnp.concatenate(
        [(buckets[k : k + 1, :] == slots).astype(f32) for k in range(kernel)], axis=0
    ).astype(bf16)
    tapped = lax.dot_general(member, spread[...], NT, preferred_element_type=f32)
    mixed = None
    for k in range(kernel):
        start = PAD - reach + k
        term = tapped[k * BUCKETS : (k + 1) * BUCKETS, start : start + patches]
        mixed = term if mixed is None else mixed + term
    hi, lo = split_in_kernel(mixed)
    both = jnp.concatenate([hi, lo], axis=0)
    for n in range(patches // POOL):
        rows = slice(n * POOL, (n + 1) * POOL)
        part = jnp.dot(both[:, rows], slope[rows, :], preferred_element_type=f32)
        kept[n] = part[:BUCKETS] + part[BUCKETS:]


def bins_stage(buckets, spread, slope):
    vmem = pl.BlockSpec(memory_space=pltpu.VMEM)
    patches, channels = slope.shape
    return pl.pallas_call(
        bins_kernel,
        out_shape=jax.ShapeDtypeStruct((patches // POOL, BUCKETS, channels), f32),
        in_specs=[vmem] * 3,
        out_specs=vmem,
        compiler_params=pltpu.CompilerParams(vmem_limit_bytes=24 << 20),
        cost_estimate=pl.CostEstimate(
            flops=400_000_000, bytes_accessed=4_000_000, transcendentals=0
        ),
        name="bins",
    )(buckets, spread, slope)


def tail_kernel(where, received, along, turned, hidden_up, inverse, kept, projection, far, near, d_pooled, sketch, edges):
    bins = kept.shape[0]
    summed = jnp.sum(received[...].astype(f32), axis=0)
    prior, later = from_sides(where, far[...], near[...])
    grads = jnp.concatenate([summed[:, : 2 * OP], summed[:, 2 * OP :]], axis=0)
    both = jnp.dot(grads, turned[...], precision=highest, preferred_element_type=f32)

    def finish(rows, grad, line, scale, lifted):
        inner = jnp.sum(grad * line, axis=1, keepdims=True)
        return (scale * rows - scale * scale * scale * inner * lifted) * (1.0 / POOL)

    scaled = finish(both[:bins], grads[:bins], along[...], inverse[:, :1], hidden_up[...])
    d_pooled[...] = scaled
    total = scaled[0:1] * kept[0]
    for n in range(1, bins):
        total = total + scaled[n : n + 1] * kept[n]
    part = jnp.dot(total, projection[...], precision=highest, preferred_element_type=f32)
    sketch[...] = jnp.broadcast_to(part[None], sketch.shape)
    first = finish(
        both[bins : bins + 1], grads[bins : bins + 1], prior[3:4, : 2 * OP], prior[4:5, :1], prior[2:3]
    )
    last = finish(
        both[2 * bins - 1 :], grads[2 * bins - 1 :], later[PAD + 3 : PAD + 4, : 2 * OP],
        later[PAD + 4 : PAD + 5, :1], later[PAD + 2 : PAD + 3],
    )
    blank = jnp.zeros((PAD - 2, first.shape[1]), f32)
    edges[...] = jnp.concatenate(
        [blank, first * prior[:2], last * later[PAD : PAD + 2], blank], axis=0
    ).astype(bf16)


def tail_stage(where, received, along, turned, hidden_up, inverse, kept, projection, far, near, fan):
    vmem = pl.BlockSpec(memory_space=pltpu.VMEM)
    bins, channels = hidden_up.shape
    return pl.pallas_call(
        tail_kernel,
        out_shape=[
            jax.ShapeDtypeStruct((bins, channels), f32),
            jax.ShapeDtypeStruct((fan, kept.shape[1], projection.shape[1]), f32),
            jax.ShapeDtypeStruct((2 * PAD, channels), bf16),
        ],
        in_specs=[pl.BlockSpec(memory_space=pltpu.SMEM)] + [vmem] * 9,
        out_specs=[vmem] * 3,
        compiler_params=pltpu.CompilerParams(vmem_limit_bytes=24 << 20),
        cost_estimate=pl.CostEstimate(flops=20_000_000, bytes_accessed=4_000_000, transcendentals=0),
        name="tail",
    )(where, received, along, turned, hidden_up, inverse, kept, projection, far, near)


def to_sides(value, axes):
    count = lax.axis_size(axes)
    inside = [(i, i ^ 1) for i in range(count)]
    across = [(0, 0), (count - 1, count - 1)] + [
        (i, i + 1 if i % 2 else i - 1) for i in range(1, count - 1)
    ]
    far = lax.ppermute(value, axes, across)
    near = lax.ppermute(value, axes, inside)
    return far, near


def one_hot(bases):
    return (
        (bases[:, :, None] == jnp.arange(4, dtype=jnp.int32))
        .astype(bf16)
        .reshape(bases.shape[0], PATCH * 4)
    )


def exchange(value, axes):
    return lax.all_to_all(value, axes, 0, 0, tiled=True)


def whole(
    tokens,
    stem_weight,
    conv_weight,
    conv_bias,
    up_weight,
    norm_gain,
    pair_weight,
    out_weight,
    cotangent,
    projection,
    buckets,
):
    channels = conv_weight.shape[1]
    kernel = conv_weight.shape[0] // channels
    reach = (kernel - 1) // 2
    line = ("seq", "col")
    count = lax.axis_size(line)
    place = lax.axis_index(line)
    where = jnp.stack(
        [lax.axis_index("seq"), lax.axis_index("col"), place, count + 0 * place]
    ).astype(jnp.int32)

    edge = reach * PATCH
    rims = one_hot(
        jnp.concatenate([tokens[0, -edge:], tokens[0, :edge]]).reshape(2 * reach, PATCH)
    )
    rims = jnp.pad(rims, ((PAD - reach, PAD - reach), (0, 0)))
    far, near = to_sides(rims, line)
    pair = pair_weight.T
    spread, slope, parts, hidden, inverse, rim = forward_stage(
        where, tokens[0].reshape(-1, LANES), far, near, stem_weight, conv_weight, conv_bias,
        up_weight, norm_gain, pair, count,
    )
    parts = exchange(parts, line)
    turned, hidden_up, along, shared, wide = weights_stage(
        hidden, inverse, rim, pair, norm_gain, up_weight, out_weight
    )
    sent = pair_stage(where, parts, cotangent[0], wide)
    received = exchange(sent, line)
    far, near = to_sides(shared, line)
    kept = bins_stage(buckets.reshape(kernel, channels), spread, slope)
    d_pooled, sketch, grad_ends = tail_stage(
        where, received, along, turned, hidden_up, inverse, kept, projection, far, near,
        lax.axis_size("seq"),
    )
    sketch = jnp.sum(exchange(sketch, "seq"), axis=0)
    input_grad = input_stage(slope, d_pooled, grad_ends, conv_weight)
    col_count = lax.axis_size("col")
    batches = lax.axis_size("batch")
    every = exchange(
        jnp.broadcast_to(sketch[None], (batches * col_count,) + sketch.shape), ("batch", "col")
    )
    sketches = jnp.sum(every.reshape(batches, col_count, *sketch.shape), axis=1)
    units = sketches * lax.rsqrt(
        jnp.mean(sketches * sketches, axis=(1, 2), keepdims=True) + 1e-06
    )
    own = lax.dynamic_slice_in_dim(units, lax.axis_index("batch"), 1, 0)
    embedding = own - jnp.sum(units, axis=0, keepdims=True) / batches
    return (input_grad[None], embedding)


def solution(mesh):
    in_specs = (
        P("batch", ("seq", "col")),
        P(),
        P(),
        P(),
        P(),
        P(),
        P(),
        P(),
        P("batch", "seq", "col", None),
        P(),
        P(),
    )
    out_specs = (P("batch", ("seq", "col"), None), P("batch", None, None))
    return jax.shard_map(whole, mesh=mesh, in_specs=in_specs, out_specs=out_specs, check_vma=False)
```

```python
import functools
import jax
import jax.numpy as jnp
from jax import lax
from jax.experimental import pallas as pl
from jax.experimental.pallas import tpu as pltpu
from jax.sharding import PartitionSpec as P


OP = 32
PATCH = 16
POOL = 128
BUCKETS = 32
LANES = 128
PAD = 8
ROOT = 0.7978845608028654
CUBIC = 0.044715

f32 = jnp.float32
bf16 = jnp.bfloat16
NT = (((1,), (1,)), ((), ()))
highest = lax.Precision.HIGHEST
HBM = pl.BlockSpec(memory_space=pl.ANY)
FULL = 67_000_000
MOST = 60 * 1024 * 1024


def split_in_kernel(x):
    hi = x.astype(bf16)
    return hi, (x - hi.astype(f32)).astype(bf16)


def pair_kernel(where, parts_in, cot_in, wide_in, out, moved, placed, parts, cot, wide, sems):
    copies = [
        pltpu.make_async_copy(source, here, sems.at[j])
        for j, (source, here) in enumerate(((parts_in, parts), (wide_in, wide), (cot_in, cot)))
    ]
    for copy in copies:
        copy.start()
    for copy in copies[:2]:
        copy.wait()
    rows, cols, _ = cot.shape
    bins = parts.shape[1]
    seq, col = where[0], where[1]
    mine = parts[pl.ds(seq * (rows // bins), rows // bins)].astype(f32).reshape(rows, LANES)
    left = mine[:, :OP].astype(bf16)
    other = parts[pl.ds(col * (cols // bins), cols // bins)].astype(f32).reshape(cols, LANES)
    right = other.T[OP : 2 * OP].astype(bf16)
    weighted = jnp.dot(left, wide[...], preferred_element_type=f32)
    for l in range(OP):
        moved[pl.ds(l, rows, stride=OP), :] = weighted[:, l * LANES : (l + 1) * LANES]
    copies[2].wait()
    grid = jnp.concatenate([cot[i] for i in range(rows)], axis=1)
    stacked = jnp.concatenate([moved[i * OP : (i + 1) * OP, :] for i in range(rows)], axis=1)
    hi, lo = split_in_kernel(stacked)
    both = lax.dot_general(
        grid, jnp.concatenate([hi, lo], axis=0), NT, preferred_element_type=f32
    )
    grad_right = both[:, :OP] + both[:, OP:]
    summed = jnp.dot(right, grid, preferred_element_type=f32)
    for i in range(rows):
        moved[i * OP : (i + 1) * OP, :] = summed[:, i * LANES : (i + 1) * LANES]
    by_row = jnp.concatenate([moved[pl.ds(l, rows, stride=OP), :] for l in range(OP)], axis=1)
    hi, lo = split_in_kernel(by_row)
    both = lax.dot_general(
        jnp.concatenate([hi, lo], axis=0), wide[...], NT, preferred_element_type=f32
    )
    grad_left = both[:rows] + both[rows:]
    placed[...] = jnp.zeros_like(placed)
    for index, grads, lane in (
        (seq * (rows // bins), grad_left, 0),
        (col * (cols // bins), grad_right, OP),
    ):
        grads = grads.reshape(-1, bins, OP)
        many = grads.shape[0]
        own = slice(lane, lane + OP)
        beside = slice(2 * OP + lane, 3 * OP + lane)
        placed[pl.ds(index + 1, many), :, own] = grads
        placed[pl.ds(index + 2, many), :1, beside] = grads[:, bins - 1 :, :]
        placed[pl.ds(index, many), bins - 1 :, beside] = grads[:, :1, :]
    out[...] = placed[1 : 1 + out.shape[0]].astype(bf16)


def pair_stage(where, parts, cot, wide):
    vmem = pl.BlockSpec(memory_space=pltpu.VMEM)
    return pl.pallas_call(
        pair_kernel,
        out_shape=jax.ShapeDtypeStruct(parts.shape, bf16),
        in_specs=[pl.BlockSpec(memory_space=pltpu.SMEM), HBM, HBM, HBM],
        out_specs=vmem,
        scratch_shapes=[
            pltpu.VMEM((cot.shape[0] * OP, LANES), f32),
            pltpu.VMEM((parts.shape[0] + 2,) + parts.shape[1:], f32),
            pltpu.VMEM(parts.shape, bf16),
            pltpu.VMEM(cot.shape, bf16),
            pltpu.VMEM(wide.shape, bf16),
            pltpu.SemaphoreType.DMA((3,)),
        ],
        compiler_params=pltpu.CompilerParams(vmem_limit_bytes=FULL),
        cost_estimate=pl.CostEstimate(flops=200_000_000, bytes_accessed=2_000_000, transcendentals=0),
        name="pair",
    )(where, parts, cot, wide)


def iota(shape, dim): return lax.broadcasted_iota(jnp.int32, shape, dim)


def from_sides(where, far, near):
    even = where[2] % 2 == 0
    before = jnp.where(even, far, near)
    behind = jnp.where(even, near, far)
    before = jnp.where(where[2] > 0, before, jnp.zeros_like(before))
    behind = jnp.where(where[2] < where[3] - 1, behind, jnp.zeros_like(behind))
    return before, behind


def forward_kernel(chunk, where, *refs):
    sources = refs[:9]
    spread, slope, parts, hidden_out, inverse_out, rim = refs[9:15]
    tokens, far, near, stem, taps, bias, up, gain, pair = refs[15:24]
    cells, unfolded, pools, spread_here, slope_here, parts_here, sems = refs[24:]
    copies = [
        pltpu.make_async_copy(source, here, sems.at[j])
        for j, (source, here) in enumerate(zip(sources, refs[15:24]))
    ]
    for copy in copies:
        copy.start()
    patches = slope.shape[0]
    per = LANES // PATCH
    channels = stem.shape[1]
    blocks = channels // LANES
    kernel = taps.shape[0] // channels
    reach = (kernel - 1) // 2
    t = iota((patches, LANES), 0)
    lane = iota((patches, LANES), 1)
    repeat = (t // per == lane).astype(bf16)
    fold = (iota((LANES, 4 * PATCH), 0) % PATCH == iota((LANES, 4 * PATCH), 1) // 4).astype(bf16)
    copies[0].wait()
    bases = tokens[...].astype(f32).astype(bf16)
    rows = jnp.dot(repeat, bases, preferred_element_type=f32)
    own = jnp.where(lane // PATCH == t % per, rows + 1.0, 0.0).astype(bf16)
    base = jnp.dot(own, fold, preferred_element_type=f32)
    onehot = (base == (iota((patches, 4 * PATCH), 1) % 4 + 1).astype(f32)).astype(f32).astype(bf16)
    for copy in copies[1:4]:
        copy.wait()
    main = jnp.dot(onehot, stem[...], preferred_element_type=f32).astype(bf16)
    before, behind = from_sides(where, far[...].astype(f32), near[...].astype(f32))
    ends = jnp.concatenate([before[:PAD], behind[PAD:]], axis=0).astype(bf16)
    edges = jnp.dot(ends, stem[...], preferred_element_type=f32).astype(bf16)
    spread_here[:PAD, :] = edges[:PAD]
    spread_here[PAD : PAD + patches, :] = main
    spread_here[PAD + patches :, :] = edges[PAD:]
    wide = main.astype(f32)
    edges = edges.astype(f32)
    for c in range(blocks):
        at = slice(c * LANES, (c + 1) * LANES)
        cells[c, :PAD, :] = edges[:PAD, at]
        cells[c, PAD : PAD + patches, :] = wide[:, at]
        cells[c, PAD + patches :, :] = edges[PAD:, at]
    outs = [pltpu.make_async_copy(spread_here, spread, sems.at[9])]
    outs[0].start()
    for r in range(patches // chunk):
        for k in range(kernel):
            for c in range(blocks):
                start = r * chunk + PAD - reach + k
                j = (k * blocks + c) * LANES
                unfolded[r % 2, :, j : j + LANES] = cells[c, start : start + chunk, :].astype(bf16)
        if r == 0:
            copies[4].wait()
            copies[5].wait()
        before = jnp.dot(unfolded[r % 2], taps[...], preferred_element_type=f32) + bias[...].reshape(1, channels)
        square = before * before
        bent = jnp.tanh(before * (ROOT + ROOT * CUBIC * square))
        half = 0.5 * (1.0 + bent)
        after = before * half
        tilt = half + before * (0.5 - 0.5 * bent * bent) * (ROOT + 3.0 * ROOT * CUBIC * square)
        slope_here[r * chunk : (r + 1) * chunk, :] = tilt.astype(bf16)
        out = pltpu.make_async_copy(
            slope_here.at[pl.ds(r * chunk, chunk)], slope.at[pl.ds(r * chunk, chunk)], sems.at[11 + r]
        )
        out.start()
        outs.append(out)
        for n in range(chunk // POOL):
            b = r * (chunk // POOL) + n
            pools[b : b + 1, :] = jnp.sum(
                after[n * POOL : (n + 1) * POOL], axis=0, keepdims=True
            ) * (1.0 / POOL)
    rim[:PAD, :] = slope_here[:PAD, :]
    rim[PAD:, :] = slope_here[patches - PAD :, :]
    for copy in copies[6:]:
        copy.wait()
    hidden = jnp.dot(pools[...].astype(bf16), up[...], preferred_element_type=f32)
    inverse = lax.rsqrt(jnp.mean(hidden * hidden, axis=1, keepdims=True) + 1e-06)
    normed = (hidden * inverse * gain[...].reshape(1, -1)).astype(bf16)
    sides = lax.dot_general(normed, pair[...], NT, preferred_element_type=f32)
    full = jnp.concatenate([sides, jnp.zeros_like(sides)], axis=1).astype(bf16)
    parts_here[...] = jnp.broadcast_to(full[None], parts.shape)
    out = pltpu.make_async_copy(parts_here, parts, sems.at[10])
    out.start()
    outs.append(out)
    hidden_out[...] = hidden
    inverse_out[...] = jnp.broadcast_to(inverse, inverse_out.shape)
    for out in outs:
        out.wait()


def forward_stage(where, tokens, far, near, stem, taps, bias, up, gain, pair, count, chunk=512):
    vmem = pl.BlockSpec(memory_space=pltpu.VMEM)
    patches = tokens.size // PATCH
    channels = stem.shape[1]
    bins = patches // POOL
    tall = patches + 2 * PAD
    inputs = (tokens, far, near, stem, taps, bias, up, gain, pair)
    return pl.pallas_call(
        functools.partial(forward_kernel, chunk),
        out_shape=[
            jax.ShapeDtypeStruct((tall, channels), bf16),
            jax.ShapeDtypeStruct((patches, channels), bf16),
            jax.ShapeDtypeStruct((count, bins, LANES), bf16),
            jax.ShapeDtypeStruct((bins, up.shape[1]), f32),
            jax.ShapeDtypeStruct((bins, LANES), f32),
            jax.ShapeDtypeStruct((2 * PAD, channels), bf16),
        ],
        in_specs=[pl.BlockSpec(memory_space=pltpu.SMEM)] + [HBM] * 9,
        out_specs=[HBM] * 3 + [vmem] * 3,
        scratch_shapes=[pltpu.VMEM(x.shape, x.dtype) for x in inputs]
        + [
            pltpu.VMEM((channels // LANES, tall, LANES), f32),
            pltpu.VMEM((2, chunk, taps.shape[0]), bf16),
            pltpu.VMEM((bins, channels), f32),
            pltpu.VMEM((tall, channels), bf16),
            pltpu.VMEM((patches, channels), bf16),
            pltpu.VMEM((count, bins, LANES), bf16),
            pltpu.SemaphoreType.DMA((11 + patches // chunk,)),
        ],
        compiler_params=pltpu.CompilerParams(vmem_limit_bytes=FULL),
        cost_estimate=pl.CostEstimate(
            flops=6_200_000_000, bytes_accessed=14_000_000, transcendentals=800_000
        ),
        name="forward",
    )(where, *inputs)


def input_kernel(chunk, where, source, d_pooled, loose, far, near, taps_in, out, cells, shifted, taps, slope, block, sems):
    patches, channels = slope.shape
    blocks = channels // LANES
    kernel = taps.shape[0] // channels
    reach = (kernel - 1) // 2
    halves = 1
    part = patches // halves
    reads = [
        pltpu.make_async_copy(
            source.at[pl.ds(h * part, part)], slope.at[pl.ds(h * part, part)], sems.at[h]
        )
        for h in range(halves)
    ]
    copies = [
        pltpu.make_async_copy(
            taps_in.at[pl.ds(k * channels, channels)],
            taps.at[pl.ds(k * channels, channels)],
            sems.at[halves + k],
        )
        for k in range(kernel)
    ]
    for copy in reads + copies:
        copy.start()
    prior, later = from_sides(where, far[...], near[...])
    wide = 2 * OP
    sides = []
    for row, other in ((0, prior[:PAD]), (1, later[PAD:])):
        grad = finish(
            loose[row : row + 1, :], loose[2 + row : 3 + row, :wide], other[3:4, :wide],
            other[4:5, :1], other[2:3],
        )
        sides.append(grad * other[:2])
    blank = jnp.zeros((PAD - 2, channels), f32)
    above = jnp.concatenate([blank, sides[0]], axis=0)
    below = jnp.concatenate([sides[1], blank], axis=0)
    for copy in reads:
        copy.wait()
    for c in range(blocks):
        at = slice(c * LANES, (c + 1) * LANES)
        cells[c, :PAD, :] = above[:, at]
        cells[c, PAD + patches :, :] = below[:, at]
        for n in range(patches // POOL):
            low, high = n * POOL, (n + 1) * POOL
            cells[c, PAD + low : PAD + high, :] = (
                slope[low:high, at].astype(f32) * d_pooled[n : n + 1, at]
            )

    def shift(r):
        for k in range(kernel):
            start = r * chunk + PAD + reach - k
            for c in range(blocks):
                j = (k * blocks + c) * LANES
                shifted[r % 2, :, j : j + LANES] = cells[c, start : start + chunk, :].astype(bf16)

    shift(0)
    for copy in copies:
        copy.wait()
    backs = []
    for r in range(patches // chunk):
        if r > 0:
            shift(r)
        total = None
        for k in range(kernel):
            at = slice(k * channels, (k + 1) * channels)
            term = lax.dot_general(
                shifted[r % 2, :, at], taps[at, :], NT, preferred_element_type=f32
            )
            total = term if total is None else total + term
        block[r * chunk : (r + 1) * chunk, :] = total.astype(bf16)
        back = pltpu.make_async_copy(
            block.at[pl.ds(r * chunk, chunk)],
            out.at[pl.ds(r * chunk, chunk)],
            sems.at[halves + kernel + r],
        )
        back.start()
        backs.append(back)
    for back in backs:
        back.wait()


def input_stage(where, slope, d_pooled, loose, far, near, taps, chunk=512):
    vmem = pl.BlockSpec(memory_space=pltpu.VMEM)
    patches, channels = slope.shape
    kernel = taps.shape[0] // channels
    return pl.pallas_call(
        functools.partial(input_kernel, chunk),
        out_shape=jax.ShapeDtypeStruct((patches, channels), bf16),
        in_specs=[pl.BlockSpec(memory_space=pltpu.SMEM), HBM] + [vmem] * 4 + [HBM],
        out_specs=HBM,
        scratch_shapes=[
            pltpu.VMEM((channels // LANES, patches + 2 * PAD, LANES), f32),
            pltpu.VMEM((2, chunk, taps.shape[0]), bf16),
            pltpu.VMEM(taps.shape, bf16),
            pltpu.VMEM(slope.shape, bf16),
            pltpu.VMEM((patches, channels), bf16),
            pltpu.SemaphoreType.DMA((1 + kernel + patches // chunk,)),
        ],
        compiler_params=pltpu.CompilerParams(vmem_limit_bytes=MOST),
        cost_estimate=pl.CostEstimate(
            flops=6_100_000_000, bytes_accessed=10_000_000, transcendentals=0
        ),
        name="inner",
    )(where, slope, d_pooled, loose, far, near, taps)


def weights_kernel(*refs):
    turned, hidden_up, along, shared, wide = refs[7:12]
    hidden, inverse, rim, pair, gain, up, mixing = refs[12:19]
    moved, sems = refs[19:]
    copies = [
        pltpu.make_async_copy(source, here, sems.at[j])
        for j, (source, here) in enumerate(zip(refs[:7], refs[12:19]))
    ]
    for copy in copies:
        copy.start()
    for copy in copies:
        copy.wait()
    _, width = up.shape
    bins = hidden.shape[0]
    scaled = pair[...].astype(f32) * gain[...].reshape(1, width)
    near = lax.dot_general(
        hidden[...], scaled, NT, precision=highest, preferred_element_type=f32
    ) * (1.0 / width)
    along[...] = near
    scaled_hi, scaled_lo = split_in_kernel(scaled)
    hidden_hi, hidden_lo = split_in_kernel(hidden[...])
    stacked = jnp.concatenate(
        [scaled_hi.astype(f32), scaled_lo.astype(f32), hidden_hi.astype(f32), hidden_lo.astype(f32)],
        axis=0,
    ).astype(bf16)
    through = lax.dot_general(stacked, up[...], NT, preferred_element_type=f32)
    turned[...] = through[: 2 * OP] + through[2 * OP : 4 * OP]
    lifted = through[4 * OP : 4 * OP + bins] + through[4 * OP + bins :]
    hidden_up[...] = lifted
    shared[...] = jnp.zeros_like(shared)
    for base, bin_at, row in ((0, bins - 1, 2 * PAD - 2), (PAD, 0, 0)):
        shared[base : base + 2, :] = rim[...].astype(f32)[row : row + 2]
        shared[base + 2 : base + 3, :] = lifted[bin_at : bin_at + 1]
        shared[base + 3 : base + 4, : 2 * OP] = near[bin_at : bin_at + 1]
        shared[base + 4 : base + 5, :LANES] = inverse[bin_at : bin_at + 1, :]
    moved[...] = mixing[...].astype(f32)
    for l in range(OP):
        wide[:, l * LANES : (l + 1) * LANES] = moved[pl.ds(l, OP, stride=OP), :].astype(bf16)


def weights_stage(hidden, inverse, rim, pair, gain, up, mixing):
    vmem = pl.BlockSpec(memory_space=pltpu.VMEM)
    bins, _ = hidden.shape
    channels = up.shape[0]
    inputs = (hidden, inverse, rim, pair, gain, up, mixing)
    return pl.pallas_call(
        weights_kernel,
        out_shape=[
            jax.ShapeDtypeStruct((2 * OP, channels), f32),
            jax.ShapeDtypeStruct((bins, channels), f32),
            jax.ShapeDtypeStruct((bins, 2 * OP), f32),
            jax.ShapeDtypeStruct((2 * PAD, channels), f32),
            jax.ShapeDtypeStruct((OP, OP * LANES), bf16),
        ],
        in_specs=[HBM] * 7,
        out_specs=[vmem] * 5,
        scratch_shapes=[pltpu.VMEM(x.shape, x.dtype) for x in inputs]
        + [pltpu.VMEM(mixing.shape, f32), pltpu.SemaphoreType.DMA((7,))],
        compiler_params=pltpu.CompilerParams(vmem_limit_bytes=FULL),
        cost_estimate=pl.CostEstimate(
            flops=340_000_000, bytes_accessed=3_000_000, transcendentals=0
        ),
        name="weights",
    )(*inputs)


def bins_kernel(buckets, spread, slope, kept):
    kernel, channels = buckets.shape
    patches = slope.shape[0]
    reach = (kernel - 1) // 2
    slots = iota((BUCKETS, channels), 0)
    member = jnp.concatenate(
        [(buckets[k : k + 1, :] == slots).astype(f32) for k in range(kernel)], axis=0
    ).astype(bf16)
    tapped = lax.dot_general(member, spread[...], NT, preferred_element_type=f32)
    mixed = None
    for k in range(kernel):
        start = PAD - reach + k
        term = tapped[k * BUCKETS : (k + 1) * BUCKETS, start : start + patches]
        mixed = term if mixed is None else mixed + term
    hi, lo = split_in_kernel(mixed)
    both = jnp.concatenate([hi, lo], axis=0)
    for n in range(patches // POOL):
        rows = slice(n * POOL, (n + 1) * POOL)
        part = jnp.dot(both[:, rows], slope[rows, :], preferred_element_type=f32)
        kept[n] = part[:BUCKETS] + part[BUCKETS:]


def bins_stage(buckets, spread, slope):
    vmem = pl.BlockSpec(memory_space=pltpu.VMEM)
    patches, channels = slope.shape
    return pl.pallas_call(
        bins_kernel,
        out_shape=jax.ShapeDtypeStruct((patches // POOL, BUCKETS, channels), f32),
        in_specs=[vmem] * 3,
        out_specs=vmem,
        compiler_params=pltpu.CompilerParams(vmem_limit_bytes=24 << 20),
        cost_estimate=pl.CostEstimate(
            flops=400_000_000, bytes_accessed=4_000_000, transcendentals=0
        ),
        name="bins",
    )(buckets, spread, slope)


def finish(rows, grad, line, scale, lifted):
    inner = jnp.sum(grad * line, axis=1, keepdims=True)
    return (scale * rows - scale * scale * scale * inner * lifted) * (1.0 / POOL)


def tail_kernel(received, along, turned, hidden_up, inverse, kept, projection, d_pooled, sketch, loose):
    bins = kept.shape[0]
    summed = jnp.sum(received[...].astype(f32), axis=0)
    grads = jnp.concatenate([summed[:, : 2 * OP], summed[:, 2 * OP :]], axis=0)
    both = jnp.dot(grads, turned[...], precision=highest, preferred_element_type=f32)

    scaled = finish(both[:bins], grads[:bins], along[...], inverse[:, :1], hidden_up[...])
    d_pooled[...] = scaled
    total = scaled[0:1] * kept[0]
    for n in range(1, bins):
        total = total + scaled[n : n + 1] * kept[n]
    part = jnp.dot(total, projection[...], precision=highest, preferred_element_type=f32)
    sketch[...] = jnp.broadcast_to(part.astype(bf16)[None], sketch.shape)
    loose[...] = jnp.zeros_like(loose)
    loose[:1, :] = both[bins : bins + 1]
    loose[1:2, :] = both[2 * bins - 1 :]
    loose[2:3, : 2 * OP] = grads[bins : bins + 1]
    loose[3:4, : 2 * OP] = grads[2 * bins - 1 :]


def tail_stage(received, along, turned, hidden_up, inverse, kept, projection, fan):
    vmem = pl.BlockSpec(memory_space=pltpu.VMEM)
    bins, channels = hidden_up.shape
    return pl.pallas_call(
        tail_kernel,
        out_shape=[
            jax.ShapeDtypeStruct((bins, channels), f32),
            jax.ShapeDtypeStruct((fan, kept.shape[1], projection.shape[1]), bf16),
            jax.ShapeDtypeStruct((PAD, channels), f32),
        ],
        in_specs=[vmem] * 7,
        out_specs=[vmem] * 3,
        compiler_params=pltpu.CompilerParams(vmem_limit_bytes=24 << 20),
        cost_estimate=pl.CostEstimate(flops=20_000_000, bytes_accessed=4_000_000, transcendentals=0),
        name="tail",
    )(received, along, turned, hidden_up, inverse, kept, projection)


def to_sides(value, axes):
    count = lax.axis_size(axes)
    inside = [(i, i ^ 1) for i in range(count)]
    across = [(0, 0), (count - 1, count - 1)] + [
        (i, i + 1 if i % 2 else i - 1) for i in range(1, count - 1)
    ]
    far = lax.ppermute(value, axes, across)
    near = lax.ppermute(value, axes, inside)
    return far, near


def one_hot(bases):
    return (
        (bases[:, :, None] == jnp.arange(4, dtype=jnp.int32))
        .astype(bf16)
        .reshape(bases.shape[0], PATCH * 4)
    )


def exchange(value, axes):
    return lax.all_to_all(value, axes, 0, 0, tiled=True)


def whole(
    tokens,
    stem_weight,
    conv_weight,
    conv_bias,
    up_weight,
    norm_gain,
    pair_weight,
    out_weight,
    cotangent,
    projection,
    buckets,
):
    channels = conv_weight.shape[1]
    kernel = conv_weight.shape[0] // channels
    reach = (kernel - 1) // 2
    line = ("seq", "col")
    count = lax.axis_size(line)
    place = lax.axis_index(line)
    where = jnp.stack(
        [lax.axis_index("seq"), lax.axis_index("col"), place, count + 0 * place]
    ).astype(jnp.int32)

    edge = reach * PATCH
    rims = one_hot(
        jnp.concatenate([tokens[0, -edge:], tokens[0, :edge]]).reshape(2 * reach, PATCH)
    )
    rims = jnp.pad(rims, ((PAD - reach, PAD - reach), (0, 0)))
    far, near = to_sides(rims, line)
    pair = pair_weight.T
    spread, slope, parts, hidden, inverse, rim = forward_stage(
        where, tokens[0].reshape(-1, LANES), far, near, stem_weight, conv_weight, conv_bias,
        up_weight, norm_gain, pair, count,
    )
    parts = exchange(parts, line)
    turned, hidden_up, along, shared, wide = weights_stage(
        hidden, inverse, rim, pair, norm_gain, up_weight, out_weight
    )
    sent = pair_stage(where, parts, cotangent[0], wide)
    received = exchange(sent, line)
    kept = bins_stage(buckets.reshape(kernel, channels), spread, slope)
    d_pooled, sketch, loose = tail_stage(
        received, along, turned, hidden_up, inverse, kept, projection,
        lax.axis_size(("batch", "seq", "col")),
    )
    batches = lax.axis_size("batch")
    every = exchange(sketch, ("batch", "seq", "col"))
    far, near = to_sides(shared, line)
    input_grad = input_stage(where, slope, d_pooled, loose, far, near, conv_weight)
    sketches = jnp.sum(
        every.astype(f32).reshape(batches, count, *sketch.shape[1:]), axis=1
    )
    units = sketches * lax.rsqrt(
        jnp.mean(sketches * sketches, axis=(1, 2), keepdims=True) + 1e-06
    )
    own = lax.dynamic_slice_in_dim(units, lax.axis_index("batch"), 1, 0)
    embedding = own - jnp.sum(units, axis=0, keepdims=True) / batches
    return (input_grad[None], embedding)


def solution(mesh):
    in_specs = (
        P("batch", ("seq", "col")),
        P(),
        P(),
        P(),
        P(),
        P(),
        P(),
        P(),
        P("batch", "seq", "col", None),
        P(),
        P(),
    )
    out_specs = (P("batch", ("seq", "col"), None), P("batch", None, None))
    return jax.shard_map(whole, mesh=mesh, in_specs=in_specs, out_specs=out_specs, check_vma=False)
```

```python
import functools
import jax
import jax.numpy as jnp
from jax import lax
from jax.experimental import pallas as pl
from jax.experimental.pallas import tpu as pltpu
from jax.sharding import PartitionSpec as P


OP = 32
PATCH = 16
POOL = 128
BUCKETS = 32
LANES = 128
PAD = 8
ROOT = 0.7978845608028654
CUBIC = 0.044715

f32 = jnp.float32
bf16 = jnp.bfloat16
NT = (((1,), (1,)), ((), ()))
highest = lax.Precision.HIGHEST
HBM = pl.BlockSpec(memory_space=pl.ANY)
FULL = 67_000_000


def split_in_kernel(x):
    hi = x.astype(bf16)
    return hi, (x - hi.astype(f32)).astype(bf16)


def pair_kernel(where, parts_in, cot_in, wide_in, out, moved, placed, parts, cot, wide, sems):
    copies = [
        pltpu.make_async_copy(source, here, sems.at[j])
        for j, (source, here) in enumerate(((parts_in, parts), (wide_in, wide), (cot_in, cot)))
    ]
    for copy in copies:
        copy.start()
    for copy in copies[:2]:
        copy.wait()
    rows, cols, _ = cot.shape
    bins = parts.shape[1]
    seq, col = where[0], where[1]
    mine = parts[pl.ds(seq * (rows // bins), rows // bins)].astype(f32).reshape(rows, LANES)
    left = mine[:, :OP].astype(bf16)
    other = parts[pl.ds(col * (cols // bins), cols // bins)].astype(f32).reshape(cols, LANES)
    right = other.T[OP : 2 * OP].astype(bf16)
    weighted = jnp.dot(left, wide[...], preferred_element_type=f32)
    for l in range(OP):
        moved[pl.ds(l, rows, stride=OP), :] = weighted[:, l * LANES : (l + 1) * LANES]
    copies[2].wait()
    grid = jnp.concatenate([cot[i] for i in range(rows)], axis=1)
    stacked = jnp.concatenate([moved[i * OP : (i + 1) * OP, :] for i in range(rows)], axis=1)
    hi, lo = split_in_kernel(stacked)
    both = lax.dot_general(
        grid, jnp.concatenate([hi, lo], axis=0), NT, preferred_element_type=f32
    )
    grad_right = both[:, :OP] + both[:, OP:]
    summed = jnp.dot(right, grid, preferred_element_type=f32)
    for i in range(rows):
        moved[i * OP : (i + 1) * OP, :] = summed[:, i * LANES : (i + 1) * LANES]
    by_row = jnp.concatenate([moved[pl.ds(l, rows, stride=OP), :] for l in range(OP)], axis=1)
    hi, lo = split_in_kernel(by_row)
    both = lax.dot_general(
        jnp.concatenate([hi, lo], axis=0), wide[...], NT, preferred_element_type=f32
    )
    grad_left = both[:rows] + both[rows:]
    placed[...] = jnp.zeros_like(placed)
    for index, grads, lane in (
        (seq * (rows // bins), grad_left, 0),
        (col * (cols // bins), grad_right, OP),
    ):
        grads = grads.reshape(-1, bins, OP)
        many = grads.shape[0]
        own = slice(lane, lane + OP)
        beside = slice(2 * OP + lane, 3 * OP + lane)
        placed[pl.ds(index + 1, many), :, own] = grads
        placed[pl.ds(index + 2, many), :1, beside] = grads[:, bins - 1 :, :]
        placed[pl.ds(index, many), bins - 1 :, beside] = grads[:, :1, :]
    out[...] = placed[1 : 1 + out.shape[0]].astype(bf16)


def pair_stage(where, parts, cot, wide):
    vmem = pl.BlockSpec(memory_space=pltpu.VMEM)
    return pl.pallas_call(
        pair_kernel,
        out_shape=jax.ShapeDtypeStruct(parts.shape, bf16),
        in_specs=[pl.BlockSpec(memory_space=pltpu.SMEM), HBM, HBM, HBM],
        out_specs=vmem,
        scratch_shapes=[
            pltpu.VMEM((cot.shape[0] * OP, LANES), f32),
            pltpu.VMEM((parts.shape[0] + 2,) + parts.shape[1:], f32),
            pltpu.VMEM(parts.shape, bf16),
            pltpu.VMEM(cot.shape, bf16),
            pltpu.VMEM(wide.shape, bf16),
            pltpu.SemaphoreType.DMA((3,)),
        ],
        compiler_params=pltpu.CompilerParams(vmem_limit_bytes=FULL),
        cost_estimate=pl.CostEstimate(flops=200_000_000, bytes_accessed=2_000_000, transcendentals=0),
        name="pair",
    )(where, parts, cot, wide)


def iota(shape, dim): return lax.broadcasted_iota(jnp.int32, shape, dim)


def from_sides(where, far, near):
    even = where[2] % 2 == 0
    before = jnp.where(even, far, near)
    behind = jnp.where(even, near, far)
    before = jnp.where(where[2] > 0, before, jnp.zeros_like(before))
    behind = jnp.where(where[2] < where[3] - 1, behind, jnp.zeros_like(behind))
    return before, behind


def forward_kernel(chunk, where, *refs):
    sources = refs[:9]
    spread, slope, parts, hidden_out, inverse_out, rim = refs[9:15]
    tokens, far, near, stem, taps, bias, up, gain, pair = refs[15:24]
    cells, unfolded, pools, spread_here, slope_here, parts_here, sems = refs[24:]
    copies = [
        pltpu.make_async_copy(source, here, sems.at[j])
        for j, (source, here) in enumerate(zip(sources, refs[15:24]))
    ]
    for copy in copies:
        copy.start()
    patches = slope.shape[0]
    per = LANES // PATCH
    channels = stem.shape[1]
    blocks = channels // LANES
    kernel = taps.shape[0] // channels
    reach = (kernel - 1) // 2
    t = iota((patches, LANES), 0)
    lane = iota((patches, LANES), 1)
    repeat = (t // per == lane).astype(bf16)
    fold = (iota((LANES, 4 * PATCH), 0) % PATCH == iota((LANES, 4 * PATCH), 1) // 4).astype(bf16)
    copies[0].wait()
    bases = tokens[...].astype(f32).astype(bf16)
    rows = jnp.dot(repeat, bases, preferred_element_type=f32)
    own = jnp.where(lane // PATCH == t % per, rows + 1.0, 0.0).astype(bf16)
    base = jnp.dot(own, fold, preferred_element_type=f32)
    onehot = (base == (iota((patches, 4 * PATCH), 1) % 4 + 1).astype(f32)).astype(f32).astype(bf16)
    for copy in copies[1:4]:
        copy.wait()
    main = jnp.dot(onehot, stem[...], preferred_element_type=f32).astype(bf16)
    before, behind = from_sides(where, far[...].astype(f32), near[...].astype(f32))
    ends = jnp.concatenate([before[:PAD], behind[PAD:]], axis=0).astype(bf16)
    edges = jnp.dot(ends, stem[...], preferred_element_type=f32).astype(bf16)
    spread_here[:PAD, :] = edges[:PAD]
    spread_here[PAD : PAD + patches, :] = main
    spread_here[PAD + patches :, :] = edges[PAD:]
    wide = main.astype(f32)
    edges = edges.astype(f32)
    for c in range(blocks):
        at = slice(c * LANES, (c + 1) * LANES)
        cells[c, :PAD, :] = edges[:PAD, at]
        cells[c, PAD : PAD + patches, :] = wide[:, at]
        cells[c, PAD + patches :, :] = edges[PAD:, at]
    outs = [pltpu.make_async_copy(spread_here, spread, sems.at[9])]
    outs[0].start()
    for r in range(patches // chunk):
        for k in range(kernel):
            for c in range(blocks):
                start = r * chunk + PAD - reach + k
                j = (k * blocks + c) * LANES
                unfolded[r % 2, :, j : j + LANES] = cells[c, start : start + chunk, :].astype(bf16)
        if r == 0:
            copies[4].wait()
            copies[5].wait()
        before = jnp.dot(unfolded[r % 2], taps[...], preferred_element_type=f32) + bias[...].reshape(1, channels)
        square = before * before
        bent = jnp.tanh(before * (ROOT + ROOT * CUBIC * square))
        half = 0.5 * (1.0 + bent)
        after = before * half
        tilt = half + before * (0.5 - 0.5 * bent * bent) * (ROOT + 3.0 * ROOT * CUBIC * square)
        slope_here[r * chunk : (r + 1) * chunk, :] = tilt.astype(bf16)
        out = pltpu.make_async_copy(
            slope_here.at[pl.ds(r * chunk, chunk)], slope.at[pl.ds(r * chunk, chunk)], sems.at[11 + r]
        )
        out.start()
        outs.append(out)
        for n in range(chunk // POOL):
            b = r * (chunk // POOL) + n
            pools[b : b + 1, :] = jnp.sum(
                after[n * POOL : (n + 1) * POOL], axis=0, keepdims=True
            ) * (1.0 / POOL)
    rim[:PAD, :] = slope_here[:PAD, :]
    rim[PAD:, :] = slope_here[patches - PAD :, :]
    for copy in copies[6:]:
        copy.wait()
    hidden = jnp.dot(pools[...].astype(bf16), up[...], preferred_element_type=f32)
    inverse = lax.rsqrt(jnp.mean(hidden * hidden, axis=1, keepdims=True) + 1e-06)
    normed = (hidden * inverse * gain[...].reshape(1, -1)).astype(bf16)
    sides = lax.dot_general(normed, pair[...], NT, preferred_element_type=f32)
    full = jnp.concatenate([sides, jnp.zeros_like(sides)], axis=1).astype(bf16)
    parts_here[...] = jnp.broadcast_to(full[None], parts.shape)
    out = pltpu.make_async_copy(parts_here, parts, sems.at[10])
    out.start()
    outs.append(out)
    hidden_out[...] = hidden
    inverse_out[...] = jnp.broadcast_to(inverse, inverse_out.shape)
    for out in outs:
        out.wait()


def forward_stage(where, tokens, far, near, stem, taps, bias, up, gain, pair, count, chunk=512):
    vmem = pl.BlockSpec(memory_space=pltpu.VMEM)
    patches = tokens.size // PATCH
    channels = stem.shape[1]
    bins = patches // POOL
    tall = patches + 2 * PAD
    inputs = (tokens, far, near, stem, taps, bias, up, gain, pair)
    return pl.pallas_call(
        functools.partial(forward_kernel, chunk),
        out_shape=[
            jax.ShapeDtypeStruct((tall, channels), bf16),
            jax.ShapeDtypeStruct((patches, channels), bf16),
            jax.ShapeDtypeStruct((count, bins, LANES), bf16),
            jax.ShapeDtypeStruct((bins, up.shape[1]), f32),
            jax.ShapeDtypeStruct((bins, LANES), f32),
            jax.ShapeDtypeStruct((2 * PAD, channels), bf16),
        ],
        in_specs=[pl.BlockSpec(memory_space=pltpu.SMEM)] + [HBM] * 9,
        out_specs=[HBM] * 3 + [vmem] * 3,
        scratch_shapes=[pltpu.VMEM(x.shape, x.dtype) for x in inputs]
        + [
            pltpu.VMEM((channels // LANES, tall, LANES), f32),
            pltpu.VMEM((2, chunk, taps.shape[0]), bf16),
            pltpu.VMEM((bins, channels), f32),
            pltpu.VMEM((tall, channels), bf16),
            pltpu.VMEM((patches, channels), bf16),
            pltpu.VMEM((count, bins, LANES), bf16),
            pltpu.SemaphoreType.DMA((11 + patches // chunk,)),
        ],
        compiler_params=pltpu.CompilerParams(vmem_limit_bytes=FULL),
        cost_estimate=pl.CostEstimate(
            flops=6_200_000_000, bytes_accessed=14_000_000, transcendentals=800_000
        ),
        name="forward",
    )(where, *inputs)


def input_kernel(chunk, source, d_pooled, ends, taps_in, out, cells, shifted, taps, slope, block, sems):
    patches, channels = slope.shape
    blocks = channels // LANES
    kernel = taps.shape[0] // channels
    reach = (kernel - 1) // 2
    halves = 1
    part = patches // halves
    reads = [
        pltpu.make_async_copy(
            source.at[pl.ds(h * part, part)], slope.at[pl.ds(h * part, part)], sems.at[h]
        )
        for h in range(halves)
    ]
    copies = [
        pltpu.make_async_copy(
            taps_in.at[pl.ds(k * channels, channels)],
            taps.at[pl.ds(k * channels, channels)],
            sems.at[halves + k],
        )
        for k in range(kernel)
    ]
    for copy in reads + copies:
        copy.start()
    for copy in reads:
        copy.wait()
    for c in range(blocks):
        at = slice(c * LANES, (c + 1) * LANES)
        cells[c, :PAD, :] = ends[:PAD, at].astype(f32)
        cells[c, PAD + patches :, :] = ends[PAD:, at].astype(f32)
        for n in range(patches // POOL):
            low, high = n * POOL, (n + 1) * POOL
            cells[c, PAD + low : PAD + high, :] = (
                slope[low:high, at].astype(f32) * d_pooled[n : n + 1, at]
            )

    def shift(r):
        for k in range(kernel):
            start = r * chunk + PAD + reach - k
            for c in range(blocks):
                j = (k * blocks + c) * LANES
                shifted[r % 2, :, j : j + LANES] = cells[c, start : start + chunk, :].astype(bf16)

    shift(0)
    for copy in copies:
        copy.wait()
    backs = []
    for r in range(patches // chunk):
        if r > 0:
            shift(r)
        total = None
        for k in range(kernel):
            at = slice(k * channels, (k + 1) * channels)
            term = lax.dot_general(
                shifted[r % 2, :, at], taps[at, :], NT, preferred_element_type=f32
            )
            total = term if total is None else total + term
        block[r * chunk : (r + 1) * chunk, :] = total.astype(bf16)
        back = pltpu.make_async_copy(
            block.at[pl.ds(r * chunk, chunk)],
            out.at[pl.ds(r * chunk, chunk)],
            sems.at[halves + kernel + r],
        )
        back.start()
        backs.append(back)
    for back in backs:
        back.wait()


def input_stage(slope, d_pooled, ends, taps, chunk=512):
    vmem = pl.BlockSpec(memory_space=pltpu.VMEM)
    patches, channels = slope.shape
    kernel = taps.shape[0] // channels
    return pl.pallas_call(
        functools.partial(input_kernel, chunk),
        out_shape=jax.ShapeDtypeStruct((patches, channels), bf16),
        in_specs=[HBM, vmem, vmem, HBM],
        out_specs=HBM,
        scratch_shapes=[
            pltpu.VMEM((channels // LANES, patches + 2 * PAD, LANES), f32),
            pltpu.VMEM((2, chunk, taps.shape[0]), bf16),
            pltpu.VMEM(taps.shape, bf16),
            pltpu.VMEM(slope.shape, bf16),
            pltpu.VMEM((patches, channels), bf16),
            pltpu.SemaphoreType.DMA((1 + kernel + patches // chunk,)),
        ],
        compiler_params=pltpu.CompilerParams(vmem_limit_bytes=36 << 20),
        cost_estimate=pl.CostEstimate(
            flops=6_100_000_000, bytes_accessed=10_000_000, transcendentals=0
        ),
        name="inner",
    )(slope, d_pooled, ends, taps)


def weights_kernel(*refs):
    turned, hidden_up, along, shared, wide = refs[7:12]
    hidden, inverse, rim, pair, gain, up, mixing = refs[12:19]
    moved, sems = refs[19:]
    copies = [
        pltpu.make_async_copy(source, here, sems.at[j])
        for j, (source, here) in enumerate(zip(refs[:7], refs[12:19]))
    ]
    for copy in copies:
        copy.start()
    for copy in copies:
        copy.wait()
    _, width = up.shape
    bins = hidden.shape[0]
    scaled = pair[...].astype(f32) * gain[...].reshape(1, width)
    near = lax.dot_general(
        hidden[...], scaled, NT, precision=highest, preferred_element_type=f32
    ) * (1.0 / width)
    along[...] = near
    scaled_hi, scaled_lo = split_in_kernel(scaled)
    hidden_hi, hidden_lo = split_in_kernel(hidden[...])
    stacked = jnp.concatenate(
        [scaled_hi.astype(f32), scaled_lo.astype(f32), hidden_hi.astype(f32), hidden_lo.astype(f32)],
        axis=0,
    ).astype(bf16)
    through = lax.dot_general(stacked, up[...], NT, preferred_element_type=f32)
    turned[...] = through[: 2 * OP] + through[2 * OP : 4 * OP]
    lifted = through[4 * OP : 4 * OP + bins] + through[4 * OP + bins :]
    hidden_up[...] = lifted
    shared[...] = jnp.zeros_like(shared)
    for base, bin_at, row in ((0, bins - 1, 2 * PAD - 2), (PAD, 0, 0)):
        shared[base : base + 2, :] = rim[...].astype(f32)[row : row + 2]
        shared[base + 2 : base + 3, :] = lifted[bin_at : bin_at + 1]
        shared[base + 3 : base + 4, : 2 * OP] = near[bin_at : bin_at + 1]
        shared[base + 4 : base + 5, :LANES] = inverse[bin_at : bin_at + 1, :]
    moved[...] = mixing[...].astype(f32)
    for l in range(OP):
        wide[:, l * LANES : (l + 1) * LANES] = moved[pl.ds(l, OP, stride=OP), :].astype(bf16)


def weights_stage(hidden, inverse, rim, pair, gain, up, mixing):
    vmem = pl.BlockSpec(memory_space=pltpu.VMEM)
    bins, _ = hidden.shape
    channels = up.shape[0]
    inputs = (hidden, inverse, rim, pair, gain, up, mixing)
    return pl.pallas_call(
        weights_kernel,
        out_shape=[
            jax.ShapeDtypeStruct((2 * OP, channels), f32),
            jax.ShapeDtypeStruct((bins, channels), f32),
            jax.ShapeDtypeStruct((bins, 2 * OP), f32),
            jax.ShapeDtypeStruct((2 * PAD, channels), f32),
            jax.ShapeDtypeStruct((OP, OP * LANES), bf16),
        ],
        in_specs=[HBM] * 7,
        out_specs=[vmem] * 5,
        scratch_shapes=[pltpu.VMEM(x.shape, x.dtype) for x in inputs]
        + [pltpu.VMEM(mixing.shape, f32), pltpu.SemaphoreType.DMA((7,))],
        compiler_params=pltpu.CompilerParams(vmem_limit_bytes=FULL),
        cost_estimate=pl.CostEstimate(
            flops=340_000_000, bytes_accessed=3_000_000, transcendentals=0
        ),
        name="weights",
    )(*inputs)


def bins_kernel(buckets, spread, slope, kept):
    kernel, channels = buckets.shape
    patches = slope.shape[0]
    reach = (kernel - 1) // 2
    slots = iota((BUCKETS, channels), 0)
    member = jnp.concatenate(
        [(buckets[k : k + 1, :] == slots).astype(f32) for k in range(kernel)], axis=0
    ).astype(bf16)
    tapped = lax.dot_general(member, spread[...], NT, preferred_element_type=f32)
    mixed = None
    for k in range(kernel):
        start = PAD - reach + k
        term = tapped[k * BUCKETS : (k + 1) * BUCKETS, start : start + patches]
        mixed = term if mixed is None else mixed + term
    hi, lo = split_in_kernel(mixed)
    both = jnp.concatenate([hi, lo], axis=0)
    for n in range(patches // POOL):
        rows = slice(n * POOL, (n + 1) * POOL)
        part = jnp.dot(both[:, rows], slope[rows, :], preferred_element_type=f32)
        kept[n] = part[:BUCKETS] + part[BUCKETS:]


def bins_stage(buckets, spread, slope):
    vmem = pl.BlockSpec(memory_space=pltpu.VMEM)
    patches, channels = slope.shape
    return pl.pallas_call(
        bins_kernel,
        out_shape=jax.ShapeDtypeStruct((patches // POOL, BUCKETS, channels), f32),
        in_specs=[vmem] * 3,
        out_specs=vmem,
        compiler_params=pltpu.CompilerParams(vmem_limit_bytes=24 << 20),
        cost_estimate=pl.CostEstimate(
            flops=400_000_000, bytes_accessed=4_000_000, transcendentals=0
        ),
        name="bins",
    )(buckets, spread, slope)


def tail_kernel(where, received, along, turned, hidden_up, inverse, kept, projection, far, near, d_pooled, sketch, edges):
    bins = kept.shape[0]
    summed = jnp.sum(received[...].astype(f32), axis=0)
    prior, later = from_sides(where, far[...], near[...])
    grads = jnp.concatenate([summed[:, : 2 * OP], summed[:, 2 * OP :]], axis=0)
    both = jnp.dot(grads, turned[...], precision=highest, preferred_element_type=f32)

    def finish(rows, grad, line, scale, lifted):
        inner = jnp.sum(grad * line, axis=1, keepdims=True)
        return (scale * rows - scale * scale * scale * inner * lifted) * (1.0 / POOL)

    scaled = finish(both[:bins], grads[:bins], along[...], inverse[:, :1], hidden_up[...])
    d_pooled[...] = scaled
    total = scaled[0:1] * kept[0]
    for n in range(1, bins):
        total = total + scaled[n : n + 1] * kept[n]
    part = jnp.dot(total, projection[...], precision=highest, preferred_element_type=f32)
    sketch[...] = jnp.broadcast_to(part.astype(bf16)[None], sketch.shape)
    first = finish(
        both[bins : bins + 1], grads[bins : bins + 1], prior[3:4, : 2 * OP], prior[4:5, :1], prior[2:3]
    )
    last = finish(
        both[2 * bins - 1 :], grads[2 * bins - 1 :], later[PAD + 3 : PAD + 4, : 2 * OP],
        later[PAD + 4 : PAD + 5, :1], later[PAD + 2 : PAD + 3],
    )
    blank = jnp.zeros((PAD - 2, first.shape[1]), f32)
    edges[...] = jnp.concatenate(
        [blank, first * prior[:2], last * later[PAD : PAD + 2], blank], axis=0
    ).astype(bf16)


def tail_stage(where, received, along, turned, hidden_up, inverse, kept, projection, far, near, fan):
    vmem = pl.BlockSpec(memory_space=pltpu.VMEM)
    bins, channels = hidden_up.shape
    return pl.pallas_call(
        tail_kernel,
        out_shape=[
            jax.ShapeDtypeStruct((bins, channels), f32),
            jax.ShapeDtypeStruct((fan, kept.shape[1], projection.shape[1]), bf16),
            jax.ShapeDtypeStruct((2 * PAD, channels), bf16),
        ],
        in_specs=[pl.BlockSpec(memory_space=pltpu.SMEM)] + [vmem] * 9,
        out_specs=[vmem] * 3,
        compiler_params=pltpu.CompilerParams(vmem_limit_bytes=24 << 20),
        cost_estimate=pl.CostEstimate(flops=20_000_000, bytes_accessed=4_000_000, transcendentals=0),
        name="tail",
    )(where, received, along, turned, hidden_up, inverse, kept, projection, far, near)


def to_sides(value, axes):
    count = lax.axis_size(axes)
    inside = [(i, i ^ 1) for i in range(count)]
    across = [(0, 0), (count - 1, count - 1)] + [
        (i, i + 1 if i % 2 else i - 1) for i in range(1, count - 1)
    ]
    far = lax.ppermute(value, axes, across)
    near = lax.ppermute(value, axes, inside)
    return far, near


def one_hot(bases):
    return (
        (bases[:, :, None] == jnp.arange(4, dtype=jnp.int32))
        .astype(bf16)
        .reshape(bases.shape[0], PATCH * 4)
    )


def exchange(value, axes):
    return lax.all_to_all(value, axes, 0, 0, tiled=True)


def whole(
    tokens,
    stem_weight,
    conv_weight,
    conv_bias,
    up_weight,
    norm_gain,
    pair_weight,
    out_weight,
    cotangent,
    projection,
    buckets,
):
    channels = conv_weight.shape[1]
    kernel = conv_weight.shape[0] // channels
    reach = (kernel - 1) // 2
    line = ("seq", "col")
    count = lax.axis_size(line)
    place = lax.axis_index(line)
    where = jnp.stack(
        [lax.axis_index("seq"), lax.axis_index("col"), place, count + 0 * place]
    ).astype(jnp.int32)

    edge = reach * PATCH
    rims = one_hot(
        jnp.concatenate([tokens[0, -edge:], tokens[0, :edge]]).reshape(2 * reach, PATCH)
    )
    rims = jnp.pad(rims, ((PAD - reach, PAD - reach), (0, 0)))
    far, near = to_sides(rims, line)
    pair = pair_weight.T
    spread, slope, parts, hidden, inverse, rim = forward_stage(
        where, tokens[0].reshape(-1, LANES), far, near, stem_weight, conv_weight, conv_bias,
        up_weight, norm_gain, pair, count,
    )
    parts = exchange(parts, line)
    turned, hidden_up, along, shared, wide = weights_stage(
        hidden, inverse, rim, pair, norm_gain, up_weight, out_weight
    )
    sent = pair_stage(where, parts, cotangent[0], wide)
    received = exchange(sent, line)
    far, near = to_sides(shared, line)
    kept = bins_stage(buckets.reshape(kernel, channels), spread, slope)
    d_pooled, sketch, grad_ends = tail_stage(
        where, received, along, turned, hidden_up, inverse, kept, projection, far, near,
        lax.axis_size(("batch", "seq", "col")),
    )
    batches = lax.axis_size("batch")
    every = exchange(sketch, ("batch", "seq", "col"))
    input_grad = input_stage(slope, d_pooled, grad_ends, conv_weight)
    sketches = jnp.sum(
        every.astype(f32).reshape(batches, count, *sketch.shape[1:]), axis=1
    )
    units = sketches * lax.rsqrt(
        jnp.mean(sketches * sketches, axis=(1, 2), keepdims=True) + 1e-06
    )
    own = lax.dynamic_slice_in_dim(units, lax.axis_index("batch"), 1, 0)
    embedding = own - jnp.sum(units, axis=0, keepdims=True) / batches
    return (input_grad[None], embedding)


def solution(mesh):
    in_specs = (
        P("batch", ("seq", "col")),
        P(),
        P(),
        P(),
        P(),
        P(),
        P(),
        P(),
        P("batch", "seq", "col", None),
        P(),
        P(),
    )
    out_specs = (P("batch", ("seq", "col"), None), P("batch", None, None))
    return jax.shard_map(whole, mesh=mesh, in_specs=in_specs, out_specs=out_specs, check_vma=False)
```
